32 devices in a mesh: ctx: 8 (over y, x, core), head: 4 (over z).
Axes of the slice: x: 2, y: 2, z: 4, core: 2. Of those that a mesh axis runs over, the one named last changes fastest.
Arguments:
- lin_q: bfloat16 [2048, 512], P('ctx', 'head'), may hold values from -6 to 6
- lin_k: bfloat16 [2048, 512], P('ctx', 'head'), may hold values from -6 to 6
- lin_v: bfloat16 [2048, 512], P('ctx', 'head'), may hold values from -6 to 6
- lin_do: bfloat16 [2048, 512], P('ctx', 'head'), may hold values from -6 to 6
- soft_q: bfloat16 [2048, 512], P('ctx', 'head'), may hold values from -7.5 to 7.5
- soft_k: bfloat16 [2048, 128], P('ctx'), may hold values from -6 to 6
- soft_v: bfloat16 [2048, 128], P('ctx'), may hold values from -6 to 6
- soft_do: bfloat16 [2048, 512], P('ctx', 'head'), may hold values from -6 to 6
- tile_list: int32 [16, 16], replicated, may hold values from 0 to 15, as said below
- tile_count: int32 [16], replicated, may hold values from 1 to 16, as said below
Outputs:
- lin_out: bfloat16 [2048, 512], P('ctx', 'head')
- lin_dq: bfloat16 [2048, 512], P('ctx', 'head')
- lin_dk: bfloat16 [2048, 512], P('ctx', 'head')
- lin_dv: bfloat16 [2048, 512], P('ctx', 'head')
- soft_out: bfloat16 [2048, 512], P('ctx', 'head')
- soft_dq: bfloat16 [2048, 512], P('ctx', 'head')
- soft_dk: bfloat16 [2048, 128], P('ctx')
- soft_dv: bfloat16 [2048, 128], P('ctx')
The draws below stay inside these ranges and needn't reach their ends.
Inputs may be any that keep to these rules, and one draw needn't show every extreme that they name: `tile_list`: row b lists distinct key blocks; its first tile_count[b] entries are b itself and then blocks below b; the other entries are 0. tile_count[b] <= b + 1; the last query block lists 16 blocks.
All inputs are finite; a program needn't handle non-finite values.
Results may differ from the reference program's by a relative error of at most 0.025.
Values may be sent and summed in bfloat16 or wider, within the bound.
A program may use at most 64 MiB of HBM per device.

```python
import math
import jax
import jax.numpy as jnp
from jax import lax

DH = 128
HEADS = 4
TOK_DEV = 256
TOKENS = 2048
TILE = 128
MAXT = 16


def draw_soft_q(key, part):
    own_key = jax.random.fold_in(key, 1)
    base = jnp.clip(jax.random.normal(own_key, (TOKENS, HEADS * DH), jnp.float32), -6.0, 6.0)
    return base.astype(jnp.bfloat16)


def draw_soft_k(key, part):
    own_key = jax.random.fold_in(key, 2)
    base = jnp.clip(jax.random.normal(own_key, (TOKENS, DH), jnp.float32), -6.0, 6.0)
    return base.astype(jnp.bfloat16)


def tile_pattern(key):
    block_total = TOKENS // TILE
    blocks = jnp.arange(block_total, dtype=jnp.int32)
    extra = jax.random.randint(jax.random.fold_in(key, 11), (block_total,), 0, MAXT // 2 + 1)
    counts = jnp.clip(1 + blocks * MAXT // block_total + extra, 1, jnp.minimum(blocks + 1, MAXT))
    counts = jnp.where(blocks == block_total - 1, MAXT, counts).astype(jnp.int32)
    column = blocks[None, :]
    row_ids = blocks[:, None]
    scores = jax.random.randint(jax.random.fold_in(key, 12), (block_total, block_total), 0, 1 << 20) * block_total + column
    scores = jnp.where(column < row_ids, scores, -1 - column)
    scores = jnp.where(column == row_ids, 1 << 30, scores)
    picked = lax.top_k(scores, MAXT)[1]
    listed = jnp.where(jnp.arange(MAXT)[None, :] < counts[:, None], picked, 0).astype(jnp.int32)
    return (listed, counts)


def draw_tile_list(key, part):
    return tile_pattern(key)[0]


def draw_tile_count(key, part):
    return tile_pattern(key)[1]


def steps_of(stream_key, extent, shards, least, largest):
    def one(dim, parts):
        steps = jax.random.uniform(jax.random.fold_in(jax.random.fold_in(stream_key, 6), dim), (parts,), jnp.float32, least / len(shards), largest / len(shards))
        return jnp.repeat(jnp.exp(steps), extent[dim] // parts).reshape((-1,) + (1,) * (len(extent) - dim - 1))

    level = one(*shards[0])
    for cut in shards[1:]:
        level = level * one(*cut)
    return level


def noise(stream_key, shape, scale, limit, shards=(), kind=jnp.bfloat16):
    drawn = jax.random.normal(stream_key, shape, jnp.float32) * scale
    if len(shards) > 0:
        drawn = steps_of(stream_key, shape, shards, -0.22, 0.18) * drawn
    return jnp.clip(drawn, min=-limit, max=limit).astype(kind)


def setup_inputs(seed: int = 0) -> dict:
    arg_keys = jax.random.split(jax.random.key(seed), 11)
    return {
        "lin_q": noise(arg_keys[0], (TOKENS, HEADS * DH), 1.0, 6.0, ((0, 8), (1, 4))),
        "lin_k": noise(arg_keys[1], (TOKENS, HEADS * DH), 1.0, 6.0, ((0, 8), (1, 4))),
        "lin_v": noise(arg_keys[2], (TOKENS, HEADS * DH), 1.0, 6.0, ((0, 8), (1, 4))),
        "lin_do": noise(arg_keys[3], (TOKENS, HEADS * DH), 1.0, 6.0, ((0, 8), (1, 4))),
        "soft_q": draw_soft_q(jax.random.fold_in(arg_keys[10], 71), 0),
        "soft_k": draw_soft_k(jax.random.fold_in(arg_keys[10], 71), 0),
        "soft_v": noise(arg_keys[6], (TOKENS, DH), 1.0, 6.0, ((0, 8),)),
        "soft_do": noise(arg_keys[7], (TOKENS, HEADS * DH), 1.0, 6.0, ((0, 8), (1, 4))),
        "tile_list": draw_tile_list(jax.random.fold_in(arg_keys[10], 71), 0),
        "tile_count": draw_tile_count(jax.random.fold_in(arg_keys[10], 71), 0),
    }


def halve(values_in):
    return lax.optimization_barrier(values_in.astype(jnp.bfloat16)).astype(jnp.float32)

def sparse_block(query_rows, cot_rows, key_all, value_all, tile_rows, count_rows, first_block):
    block_count = tile_rows.shape[0]
    slot_count = tile_rows.shape[1]
    head_width = query_rows.shape[1]
    total_blocks = key_all.shape[0] // TILE
    inverse_square_root = 1.0 / math.sqrt(head_width)
    key_tile_group = key_all.reshape(total_blocks, TILE, head_width)[tile_rows].astype(jnp.float32)
    value_tile_group = value_all.reshape(total_blocks, TILE, head_width)[tile_rows].astype(jnp.float32)
    query_block_list = query_rows.reshape(block_count, TILE, head_width).astype(jnp.float32)
    cotangent_block_list = cot_rows.reshape(block_count, TILE, head_width).astype(jnp.float32)
    logit_scores = jnp.einsum('urh,uawh->uraw', query_block_list, key_tile_group) * inverse_square_root
    slot_live = jnp.arange(slot_count, dtype=jnp.int32)[None, :] < count_rows[:, None]
    diagonal = tile_rows == (first_block + jnp.arange(block_count, dtype=jnp.int32))[:, None]
    causal = jnp.arange(TILE)[None, :] <= jnp.arange(TILE)[:, None]
    allowed = slot_live[:, None, :, None] & (jnp.logical_not(diagonal)[:, None, :, None] | causal[None, :, None, :])
    logit_scores = jnp.where(allowed, logit_scores, -jnp.inf)
    row_max = lax.optimization_barrier(jnp.max(logit_scores, axis=(2, 3), keepdims=True))
    weights = jnp.exp(logit_scores - row_max)
    soft_probs = weights / lax.optimization_barrier(jnp.sum(weights, axis=(2, 3), keepdims=True))
    probability_half_width = halve(soft_probs)
    output_blocks = jnp.einsum('mahi,mhil->mal', probability_half_width, value_tile_group).astype(jnp.bfloat16)
    row_delta = lax.optimization_barrier(jnp.sum(cotangent_block_list * output_blocks.astype(jnp.float32), axis=2))
    probability_gradient = jnp.einsum('urh,uawh->uraw', cotangent_block_list, value_tile_group)
    logit_gradient = halve(soft_probs * (probability_gradient - row_delta[:, :, None, None]) * inverse_square_root)
    query_gradient_blocks = jnp.einsum('mahi,mhil->mal', logit_gradient, key_tile_group).astype(jnp.bfloat16)
    key_summands = jnp.einsum('elmf,elo->emfo', logit_gradient, query_block_list)
    value_summands = jnp.einsum('elmf,elo->emfo', probability_half_width, cotangent_block_list)
    flat_tiles = tile_rows.reshape(-1)
    key_grad = jnp.zeros((total_blocks, TILE, head_width), jnp.float32).at[flat_tiles].add(key_summands.reshape(-1, TILE, head_width))
    value_grad = jnp.zeros((total_blocks, TILE, head_width), jnp.float32).at[flat_tiles].add(value_summands.reshape(-1, TILE, head_width))
    return (output_blocks.reshape(-1, head_width), query_gradient_blocks.reshape(-1, head_width), key_grad.reshape(-1, head_width), value_grad.reshape(-1, head_width))

def linear_head(operands):
    head_query, head_key, head_value, head_cot = operands
    length = head_query.shape[0]
    seg_count = length // TOK_DEV
    positions = jnp.arange(length, dtype=jnp.int32)
    row_scale = 1.0 / jnp.sqrt(DH * (positions + 1).astype(jnp.float32))
    scaled_cot = (head_cot.astype(jnp.float32) * row_scale[:, None]).astype(jnp.bfloat16)

    def segments(values_in):
        return values_in.reshape(seg_count, TOK_DEV, DH).astype(jnp.float32)
    seg_q = segments(head_query)
    seg_k = segments(head_key)
    seg_v = segments(head_value)
    seg_c = segments(scaled_cot)
    highest = lax.Precision.HIGHEST
    key_state = jnp.einsum('btd,bte->bde', seg_k, seg_v)
    query_state = jnp.einsum('btd,bte->bde', seg_q, seg_c)
    zero_state = jnp.zeros((1, DH, DH), jnp.float32)
    prefix = jnp.concatenate([zero_state, jnp.cumsum(key_state, axis=0)[:-1]], axis=0)
    suffix = jnp.concatenate([jnp.cumsum(query_state[::-1], axis=0)[::-1][1:], zero_state], axis=0)
    lower_tri = jnp.arange(TOK_DEV)[:, None] >= jnp.arange(TOK_DEV)[None, :]
    attn_qk = halve(jnp.where(lower_tri, jnp.einsum('bid,bjd->bij', seg_q, seg_k), 0.0))
    attn_dv = halve(jnp.where(lower_tri, jnp.einsum('bid,bjd->bij', seg_c, seg_v), 0.0))
    seg_scale = row_scale.reshape(seg_count, TOK_DEV, 1)
    out_seg = seg_scale * (jnp.einsum('bij,bjd->bid', attn_qk, seg_v) + jnp.einsum('bid,bde->bie', seg_q, prefix, precision=highest))
    grad_q = jnp.einsum('bij,bjd->bid', attn_dv, seg_k) + jnp.einsum('bie,bde->bid', seg_c, prefix, precision=highest)
    grad_k = jnp.einsum('bij,bid->bjd', attn_dv, seg_q) + jnp.einsum('bje,bde->bjd', seg_v, suffix, precision=highest)
    grad_v = jnp.einsum('bij,bie->bje', attn_qk, seg_c) + jnp.einsum('bjd,bde->bje', seg_k, suffix, precision=highest)
    return tuple((item.reshape(length, DH).astype(jnp.bfloat16) for item in (out_seg, grad_q, grad_k, grad_v)))

def split_heads(values_in):
    return values_in.reshape(values_in.shape[0], HEADS, DH).transpose(1, 0, 2)

def join_heads(values_in):
    return values_in.transpose(1, 0, 2).reshape(values_in.shape[1], HEADS * DH)

def reference(lin_q, lin_k, lin_v, lin_do, soft_q, soft_k, soft_v, soft_do, tile_list, tile_count):
    lin_results = lax.map(linear_head, (split_heads(lin_q), split_heads(lin_k), split_heads(lin_v), split_heads(lin_do)))
    lin_out, lin_dq, lin_dk, lin_dv = [join_heads(item) for item in lin_results]
    group_count = TOKENS // TOK_DEV
    blocks_dev = TOK_DEV // TILE

    def head_step(carried, operands):
        head_query, head_cot = operands

        def group_step(inner_sums, group_idx):
            start = group_idx * TOK_DEV
            query_rows = lax.dynamic_slice_in_dim(head_query, start, TOK_DEV, 0)
            cot_rows = lax.dynamic_slice_in_dim(head_cot, start, TOK_DEV, 0)
            first_block = group_idx * blocks_dev
            tile_rows = lax.dynamic_slice_in_dim(tile_list, first_block, blocks_dev, 0)
            count_rows = lax.dynamic_slice_in_dim(tile_count, first_block, blocks_dev, 0)
            out_rows, dq_rows, key_grad, value_grad = sparse_block(query_rows, cot_rows, soft_k, soft_v, tile_rows, count_rows, first_block)
            key_sum, value_sum = inner_sums
            return ((key_sum + halve(key_grad), value_sum + halve(value_grad)), (out_rows, dq_rows))
        carried, (out_all, dq_all) = lax.scan(group_step, carried, jnp.arange(group_count, dtype=jnp.int32))
        return (carried, (out_all.reshape(TOKENS, DH), dq_all.reshape(TOKENS, DH)))
    zero_grad = jnp.zeros((TOKENS, DH), jnp.float32)
    (key_sum, value_sum), (soft_outs, soft_dqs) = lax.scan(head_step, (zero_grad, zero_grad), (split_heads(soft_q), split_heads(soft_do)))
    return (lin_out, lin_dq, lin_dk, lin_dv, join_heads(soft_outs), join_heads(soft_dqs), key_sum.astype(jnp.bfloat16), value_sum.astype(jnp.bfloat16))
```

```python
import functools
import math

import jax
import jax.numpy as jnp
from jax import lax
from jax.experimental import pallas as pl
from jax.experimental.pallas import tpu as pltpu
from jax.sharding import PartitionSpec as P

TILE = 128
BF = jnp.bfloat16
F32 = jnp.float32
MESH = pl.DeviceIdType.MESH


def mm(a, b, da, db):
    return lax.dot_general(a, b, (((da,), (db,)), ((), ())), preferred_element_type=F32)


def layer_kernel(
    n, m, head_sum,
    lq_in, lk_in, lv_in, ldo_in, sq_in, sk_in, sv_in, sdo_in, tl_in, tc_in,
    *refs,
):
    if head_sum:
        o, *refs = refs
    else:
        o, o_sd, *refs = refs
    (
        lq, lk, lv, ldo, sq, sdo, tl, tc, kv, sbuf, dpbuf, st_own, st_par, st_half, st_all,
        lin_acc, g, pin, gs, rin, hb, hin, fq, fin, tops, ins,
        kvs, kvr, fws, fwr, xs, xr, hs, hr, gps, gpr, grs, grr, zs, zr, fs, fr,
    ) = refs
    rows, d = lq.shape
    chips = n // 2
    c = lax.axis_index("ctx")
    h = lax.axis_index("head")
    p = c // 2
    k = c % 2
    other = 1 - k
    partner = (p * 2 + other, h)
    half = pl.ds(pl.multiple_of(k * rows, rows), rows)
    other_half = pl.ds(pl.multiple_of(other * rows, rows), rows)
    loads = []
    for i, (a, b) in enumerate((
        (sk_in, kv.at[p, 0, half]), (sv_in, kv.at[p, 1, half]), (lk_in, lk), (lv_in, lv),
        (lq_in, lq), (ldo_in, ldo), (tl_in, tl), (tc_in, tc), (sq_in, sq), (sdo_in, sdo),
    )):
        loads.append(pltpu.make_async_copy(a, b, ins.at[i]))
    inv = 1.0 / math.sqrt(d)

    def rcopy(src, dst, s, r, dev):
        return pltpu.make_async_remote_copy(
            src_ref=src, dst_ref=dst, send_sem=s, recv_sem=r, device_id=dev, device_id_type=MESH
        )

    for load in loads[:6]:
        load.start()
    barrier = pltpu.get_barrier_semaphore()
    for i in range(1, n):
        pl.semaphore_signal(
            barrier, inc=1, device_id=((c + i) % n, h), device_id_type=MESH
        )
    heads = m if head_sum else 1
    for i in range(1, heads):
        pl.semaphore_signal(
            barrier, inc=1, device_id=(c, (h + i) % m), device_id_type=MESH
        )

    for load in loads[6:]:
        load.start()
    for load in loads[2:6]:
        load.wait()
    pos = (c * rows + lax.broadcasted_iota(jnp.int32, (rows, d), 0) + 1).astype(F32)
    row_scale = 1.0 / jnp.sqrt(d * pos)
    scot = (ldo[...].astype(F32) * row_scale).astype(BF)
    st_own[0] = mm(lk[...], lv[...], 0, 0).astype(BF)
    st_own[1] = mm(lq[...], scot, 0, 0).astype(BF)
    loads[0].wait()
    loads[1].wait()
    pl.semaphore_wait(barrier, n - 1 + heads - 1)

    def src(t):
        return kv.at[p, t, half]

    def own_to_partner(t):
        return rcopy(src(t), kv.at[p, t, half], fws.at[p, t], fwr.at[p, t], partner)

    def own_to_chip(j, t):
        return rcopy(src(t), kv.at[p, t, half], kvs.at[j, t], kvr.at[p, t], (j * 2 + k, h))

    def from_chip(j, t):
        return rcopy(src(t), kv.at[j, t, half], kvs.at[j, t], kvr.at[j, t], (j * 2 + k, h))

    def forward(j, t):
        return rcopy(
            kv.at[j, t, half], kv.at[j, t, half], fws.at[j, t], fwr.at[j, t], partner
        )

    def from_partner(j, t):
        return rcopy(
            kv.at[j, t, half], kv.at[j, t, other_half], fws.at[j, t], fwr.at[j, t], partner
        )

    exchange = rcopy(st_own, st_par, xs, xr, partner)
    exchange.start()
    for t in range(2):
        own_to_partner(t).start()

    @pl.loop(p + 1, chips)
    def _(j):
        own_to_chip(j, 0).start()
        own_to_chip(j, 1).start()

    tri = lax.broadcasted_iota(jnp.int32, (rows, rows), 0) >= lax.broadcasted_iota(
        jnp.int32, (rows, rows), 1
    )
    aqk = jnp.where(tri, mm(lq[...], lk[...], 1, 1), 0.0).astype(BF)
    adv = jnp.where(tri, mm(scot, lv[...], 1, 1), 0.0).astype(BF)
    lin_acc[0] = mm(aqk, lv[...], 1, 0)
    lin_acc[1] = mm(adv, lk[...], 1, 0)
    lin_acc[2] = mm(adv, lq[...], 0, 0)
    lin_acc[3] = mm(aqk, scot, 0, 0)

    exchange.wait()
    st_half[...] = (st_own[...].astype(F32) + st_par[...].astype(F32)).astype(BF)
    hd = d // 2
    my_part = pl.ds(pl.multiple_of(k * hd, hd), hd)

    def state_send(j, t, kk):
        return rcopy(
            st_half.at[t, my_part], st_all.at[p, my_part], hs.at[j, kk], hr.at[p, k],
            (j * 2 + kk, h),
        )

    def state_recv(j, kk):
        part = pl.ds(kk * hd, hd)
        return rcopy(
            st_half.at[0, part], st_all.at[j, part], hs.at[j, kk], hr.at[j, kk], partner
        )

    @pl.loop(0, p)
    def _(j):
        for kk in range(2):
            state_send(j, 1, kk).start()

    @pl.loop(p + 1, chips)
    def _(j):
        for kk in range(2):
            state_send(j, 0, kk).start()

    for load in loads[6:]:
        load.wait()
    blocks = rows // TILE
    bits = []
    for b in range(blocks):
        row = c * blocks + b
        word = jnp.int32(0)
        for s in range(tl.shape[1]):
            bit = lax.shift_left(jnp.int32(1), tl[row, s])
            word = word | jnp.where(s < tc[row], bit, 0)
        bits.append(word)
    lane_block = lax.broadcasted_iota(jnp.int32, (1, rows), 1) // TILE
    factor = inv * math.log2(math.e)
    chip_rows = 2 * rows
    chip_blocks = chip_rows // TILE

    def scores(j, top, own):
        for i in range(chip_blocks):
            kb = j * chip_blocks + i
            bias = jnp.zeros((1, rows), F32)
            for b in range(blocks):
                live = lax.shift_right_logical(bits[b], kb) & 1
                bias = jnp.where(lane_block == b, jnp.where(live == 1, 0.0, -1e30), bias)
            part = pl.ds(i * TILE, TILE)
            s = mm(kv[j, 0, part], sq[...], 1, 1) * factor + bias
            if own:
                key = i * TILE + lax.broadcasted_iota(jnp.int32, (TILE, rows), 0)
                query = k * rows + lax.broadcasted_iota(jnp.int32, (TILE, rows), 1)
                s = jnp.where(key <= query, s, -1e30)
            sbuf[j, part] = s
            top = jnp.maximum(top, jnp.max(s, axis=0, keepdims=True))
        return top

    def value_scores(j):
        dpbuf[j] = mm(kv[j, 1], sdo[...], 1, 1)

    def fold(j, carry, own):
        top, total, acc = carry
        from_partner(j, 0).wait_recv()
        new_top = scores(j, top, own)
        e = jnp.exp2(sbuf[j] - new_top)
        sbuf[j] = e
        tops[j] = new_top
        alpha = jnp.exp2(top - new_top)
        total = total * alpha + jnp.sum(e, axis=0, keepdims=True)
        from_partner(j, 1).wait_recv()
        value_scores(j)
        return new_top, total, acc * alpha + mm(kv[j, 1], e.astype(BF), 0, 0)

    def arrive(step, carry):
        j = p - step
        for t in range(2):
            from_chip(j, t).wait_recv()
            forward(j, t).start()
        return fold(j, carry, False)

    carry = (
        jnp.full((1, rows), -3e30, F32), jnp.zeros((1, rows), F32), jnp.zeros((d, rows), F32)
    )
    top, total, acc = lax.fori_loop(1, p + 1, arrive, fold(p, carry, True))
    inv_total = 1.0 / total

    def to_partner(t, j):
        return rcopy(
            g.at[t, j, other_half], pin.at[t, j], gps.at[t, j], gpr.at[t, j], partner
        )

    def to_owner(t, j):
        return rcopy(
            gs.at[t, j], rin.at[t, p], grs.at[t, j], grr.at[t, p], (j * 2 + k, h)
        )

    def pass_on(t, j):
        to_partner(t, j).wait_recv()
        gs[t, j] = (g[t, j, half].astype(F32) + pin[t, j].astype(F32)).astype(BF)
        to_owner(t, j).start()

    @pl.loop(0, p + 1)
    def _(j):
        prob = sbuf[j] * (jnp.exp2(tops[j] - top) * inv_total)
        sbuf[j] = prob
        g[1, j] = mm(prob.astype(BF), sdo[...], 1, 0).astype(BF)
        to_partner(1, j).start()

    out_t = (acc * inv_total).astype(BF).astype(F32)
    delta = jnp.sum(sdo[...].astype(F32).T * out_t, axis=0, keepdims=True)

    def grads(j, dq_t):
        @pl.when(j < p)
        def _():
            pass_on(1, j)

        ds = (sbuf[j] * (dpbuf[j] - delta) * inv).astype(BF)
        g[0, j] = mm(ds, sq[...], 1, 0).astype(BF)
        to_partner(0, j).start()

        @pl.when(j >= 2)
        def _():
            pass_on(0, j - 2)

        return dq_t + mm(kv[j, 0], ds, 0, 0)

    dq_t = lax.fori_loop(0, p + 1, grads, jnp.zeros((d, rows), F32))

    @pl.when(p >= 1)
    def _():
        pass_on(0, p - 1)

    o[4] = out_t.T.astype(BF)
    o[5] = dq_t.T.astype(BF)

    kf = jnp.where(k == 1, 1.0, 0.0).astype(F32)
    prefix = st_par[0].astype(F32) * kf
    suffix = st_par[1].astype(F32) * (1.0 - kf)

    def add_state(j, v):
        for kk in range(2):
            state_recv(j, kk).wait_recv()
        return v + st_all[j].astype(F32)

    prefix = lax.fori_loop(0, p, add_state, prefix).astype(BF)
    suffix = lax.fori_loop(p + 1, chips, add_state, suffix).astype(BF)
    o[0] = (row_scale * (lin_acc[0] + mm(lq[...], prefix, 1, 0))).astype(BF)
    o[1] = (lin_acc[1] + mm(scot, prefix, 1, 1)).astype(BF)
    o[2] = (lin_acc[2] + mm(lv[...], suffix, 1, 1)).astype(BF)
    o[3] = (lin_acc[3] + mm(lk[...], suffix, 1, 0)).astype(BF)

    def owned(t):
        to_partner(t, p).wait_recv()

        def add_grad(j, v):
            rcopy(gs.at[t, j], rin.at[t, j], grs.at[t, j], grr.at[t, j], partner).wait_recv()
            return v + rin[t, j].astype(F32)

        first = g[t, p, half].astype(F32) + pin[t, p].astype(F32)
        return lax.fori_loop(p + 1, chips, add_grad, first)

    if head_sum:
        part_rows = rows // m

        def to_head(t, i):
            q = (h + i) % m
            return rcopy(hb.at[t, q], hin.at[t, h], zs.at[t, q], zr.at[t, h], (c, q))

        def from_head(t, i):
            q = (h + i) % m
            return rcopy(hb.at[t, q], hin.at[t, q], zs.at[t, q], zr.at[t, q], (c, q))

        def result_to(t, i):
            q = (h + i) % m
            return rcopy(fq.at[t], fin.at[t, h], fs.at[t, q], fr.at[t, h], (c, q))

        def result_from(t, i):
            q = (h + i) % m
            return rcopy(fq.at[t], fin.at[t, q], fs.at[t, q], fr.at[t, q], (c, q))

        for t in (1, 0):
            mine = owned(t)
            for q in range(m):
                hb[t, q] = mine[q * part_rows : (q + 1) * part_rows].astype(BF)
            for i in range(1, m):
                to_head(t, i).start()
        for t in (1, 0):
            part = hb[t, h].astype(F32)
            for i in range(1, m):
                from_head(t, i).wait_recv()
                part = part + hin[t, (h + i) % m].astype(F32)
            fq[t] = part.astype(BF)
            for i in range(1, m):
                result_to(t, i).start()
            fin[t, h] = fq[t]
        for t in (1, 0):
            for i in range(1, m):
                result_from(t, i).wait_recv()
            for q in range(m):
                o[6 + t, q * part_rows : (q + 1) * part_rows] = fin[t, q]
            for i in range(1, m):
                to_head(t, i).wait_send()
                result_to(t, i).wait_send()
    else:
        for t in (1, 0):
            o_sd[t] = owned(t)

    for t in range(2):
        own_to_partner(t).wait_send()
    for t in range(2):
        to_partner(t, p).wait_send()

    @pl.loop(0, p)
    def _(j):
        for t in range(2):
            forward(j, t).wait_send()
        for kk in range(2):
            state_send(j, 1, kk).wait_send()
        for t in range(2):
            to_partner(t, j).wait_send()
            to_owner(t, j).wait_send()

    @pl.loop(p + 1, chips)
    def _(j):
        for t in range(2):
            own_to_chip(j, t).wait_send()
        for kk in range(2):
            state_send(j, 0, kk).wait_send()


def body(n, m, lin_q, lin_k, lin_v, lin_do, soft_q, soft_k, soft_v, soft_do, tile_list, tile_count):
    rows, d = lin_q.shape
    chips = n // 2
    head_sum = rows % (16 * m) == 0
    vmem = pl.BlockSpec(memory_space=pltpu.VMEM)
    hbm = pl.BlockSpec(memory_space=pltpu.HBM)
    if head_sum:
        out_shape = (pltpu.VMEM((8, rows, d), BF),)
    else:
        out_shape = (pltpu.VMEM((6, rows, d), BF), pltpu.VMEM((2, rows, d), F32))
    args = [
        pltpu.with_memory_space_constraint(x, pltpu.HBM)
        for x in (
            lin_q, lin_k, lin_v, lin_do, soft_q, soft_k, soft_v, soft_do, tile_list, tile_count
        )
    ]
    one = pltpu.VMEM((rows, d), BF)
    pr = rows // m if head_sum else 16
    dma = pltpu.SemaphoreType.DMA
    outs = pl.pallas_call(
        functools.partial(layer_kernel, n, m, head_sum),
        name="layer",
        out_shape=out_shape,
        in_specs=[hbm] * 10,
        out_specs=(vmem,) * len(out_shape),
        scratch_shapes=[
            one, one, one, one, one, one,
            pltpu.SMEM(tile_list.shape, jnp.int32),
            pltpu.SMEM(tile_count.shape, jnp.int32),
            pltpu.VMEM((chips, 2, 2 * rows, d), BF),
            pltpu.VMEM((chips, 2 * rows, rows), F32),
            pltpu.VMEM((chips, 2 * rows, rows), F32),
            pltpu.VMEM((2, d, d), BF),
            pltpu.VMEM((2, d, d), BF),
            pltpu.VMEM((2, d, d), BF),
            pltpu.VMEM((chips, d, d), BF),
            pltpu.VMEM((4, rows, d), F32),
            pltpu.VMEM((2, chips, 2 * rows, d), BF),
            pltpu.VMEM((2, chips, rows, d), BF),
            pltpu.VMEM((2, chips, rows, d), BF),
            pltpu.VMEM((2, chips, rows, d), BF),
            pltpu.VMEM((2, m, pr, d), BF),
            pltpu.VMEM((2, m, pr, d), BF),
            pltpu.VMEM((2, pr, d), BF),
            pltpu.VMEM((2, m, pr, d), BF),
            pltpu.VMEM((chips, 1, rows), F32),
            dma((10,)),
            dma((chips, 2)), dma((chips, 2)), dma((chips, 2)), dma((chips, 2)),
            dma, dma,
            dma((chips, 2)), dma((chips, 2)),
            dma((2, chips)), dma((2, chips)), dma((2, chips)), dma((2, chips)),
            dma((2, m)), dma((2, m)), dma((2, m)), dma((2, m)),
        ],
        compiler_params=pltpu.CompilerParams(
            collective_id=0, has_side_effects=True, vmem_limit_bytes=40 << 20
        ),
    )(*args)
    if head_sum:
        return tuple(outs[0][i] for i in range(8))
    soft_d = lax.psum(outs[1], "head").astype(BF)
    return tuple(outs[0][i] for i in range(6)) + (soft_d[0], soft_d[1])


def solution(mesh):
    n, m = mesh.shape["ctx"], mesh.shape["head"]
    both = P("ctx", "head")
    seq = P("ctx", None)
    return jax.shard_map(
        functools.partial(body, n, m),
        mesh=mesh,
        in_specs=(both, both, both, both, both, seq, seq, both, P(), P()),
        out_specs=(both,) * 6 + (seq, seq),
        check_vma=False,
    )
```

```python
import functools
import math

import jax
import jax.numpy as jnp
from jax import lax
from jax.experimental import pallas as pl
from jax.experimental.pallas import tpu as pltpu
from jax.sharding import PartitionSpec as P

TILE = 128
BF = jnp.bfloat16
F32 = jnp.float32
MESH = pl.DeviceIdType.MESH


def mm(a, b, da, db):
    return lax.dot_general(a, b, (((da,), (db,)), ((), ())), preferred_element_type=F32)


def layer_kernel(
    n, m, head_sum,
    lq_in, lk_in, lv_in, ldo_in, sq_in, sk_in, sv_in, sdo_in, tl_in, tc_in,
    *refs,
):
    if head_sum:
        o, *refs = refs
    else:
        o, o_sd, *refs = refs
    (
        lq, lk, lv, ldo, sq, sdo, tl, tc, kv, sbuf, dpbuf, st_own, st_par, st_half, st_all,
        lin_acc, g, rin, acc, acc_in, dq, dq_in, stat, stat_in, g_own, hb, hin, fq, fin, fb, fbin, fsum, fsum_in, psum, tops, ins,
        kvs, kvr, ps, pr, xs, xr, hs, hr, grs, grr, zs, zr, fs, fr, fzs, fzr, fos, for_,
    ) = refs
    rows, d = lq.shape
    chips = n // 2
    c = lax.axis_index("ctx")
    h = lax.axis_index("head")
    p = c // 2
    k = c % 2
    other = 1 - k
    partner = (p * 2 + other, h)
    first = pl.ds(0, rows)
    second = pl.ds(rows, rows)
    loads = []
    for i, (a, b) in enumerate((
        (sk_in, kv.at[p, 0]), (sv_in, kv.at[p, 1]), (sq_in, sq.at[first]), (sdo_in, sdo.at[first]),
        (lk_in, lk), (lv_in, lv), (lq_in, lq), (ldo_in, ldo), (tl_in, tl), (tc_in, tc),
    )):
        loads.append(pltpu.make_async_copy(a, b, ins.at[i]))
    inv = 1.0 / math.sqrt(d)

    def rcopy(src, dst, s, r, dev):
        return pltpu.make_async_remote_copy(
            src_ref=src, dst_ref=dst, send_sem=s, recv_sem=r, device_id=dev, device_id_type=MESH
        )

    for load in loads:
        load.start()
    barrier = pltpu.get_barrier_semaphore()
    for i in range(1, n):
        pl.semaphore_signal(
            barrier, inc=1, device_id=((c + i) % n, h), device_id_type=MESH
        )
    heads = m if head_sum else 1
    for i in range(1, heads):
        pl.semaphore_signal(
            barrier, inc=1, device_id=(c, (h + i) % m), device_id_type=MESH
        )

    for load in loads[4:8]:
        load.wait()
    pos = (c * rows + lax.broadcasted_iota(jnp.int32, (rows, d), 0) + 1).astype(F32)
    row_scale = 1.0 / jnp.sqrt(d * pos)
    scot = (ldo[...].astype(F32) * row_scale).astype(BF)
    st_own[0] = mm(lk[...], lv[...], 0, 0).astype(BF)
    st_own[1] = mm(lq[...], scot, 0, 0).astype(BF)
    for load in loads[:4] + loads[8:]:
        load.wait()
    blocks = rows // TILE
    part_rows = rows // m
    bits = []
    for seg in (c, p * 2 + other):
        for b in range(blocks):
            row = seg * blocks + b
            word = jnp.int32(0)
            for s in range(tl.shape[1]):
                bit = lax.shift_left(jnp.int32(1), tl[row, s])
                word = word | jnp.where(s < tc[row], bit, 0)
            bits.append(word)
    pl.semaphore_wait(barrier, n - 1 + heads - 1)

    def to_chip(j, t):
        return rcopy(kv.at[p, t], kv.at[p, t], kvs.at[j, t], kvr.at[p, t], (j * 2 + k, h))

    def from_chip(j, t):
        return rcopy(kv.at[p, t], kv.at[j, t], kvs.at[j, t], kvr.at[j, t], (j * 2 + k, h))

    @pl.loop(p + 1, chips)
    def _(i):
        j = chips - (i - p)
        to_chip(j, 0).start()
        to_chip(j, 1).start()

    swap_q = rcopy(sq.at[first], sq.at[second], ps.at[0], pr.at[0], partner)
    swap_do = rcopy(sdo.at[first], sdo.at[second], ps.at[1], pr.at[1], partner)
    exchange = rcopy(st_own, st_par, xs, xr, partner)
    swap_q.start()
    swap_do.start()
    exchange.start()

    tri = lax.broadcasted_iota(jnp.int32, (rows, rows), 0) >= lax.broadcasted_iota(
        jnp.int32, (rows, rows), 1
    )
    aqk = jnp.where(tri, mm(lq[...], lk[...], 1, 1), 0.0).astype(BF)
    adv = jnp.where(tri, mm(scot, lv[...], 1, 1), 0.0).astype(BF)
    lin_acc[0] = mm(aqk, lv[...], 1, 0)
    lin_acc[1] = mm(adv, lk[...], 1, 0)
    lin_acc[2] = mm(adv, lq[...], 0, 0)
    lin_acc[3] = mm(aqk, scot, 0, 0)

    exchange.wait()
    st_half[...] = (st_own[...].astype(F32) + st_par[...].astype(F32)).astype(BF)
    hd = d // 2
    my_part = pl.ds(pl.multiple_of(k * hd, hd), hd)

    def state_send(j, t, kk):
        return rcopy(
            st_half.at[t, my_part], st_all.at[p, my_part], hs.at[j, kk], hr.at[p, k],
            (j * 2 + kk, h),
        )

    def state_recv(j, kk):
        part = pl.ds(kk * hd, hd)
        return rcopy(
            st_half.at[0, part], st_all.at[j, part], hs.at[j, kk], hr.at[j, kk], partner
        )

    @pl.loop(0, p)
    def _(j):
        for kk in range(2):
            state_send(j, 1, kk).start()

    both_rows = 2 * rows
    lane_block = lax.broadcasted_iota(jnp.int32, (1, both_rows), 1) // TILE
    factor = inv * math.log2(math.e)

    def fold(j, carry, own):
        top, total = carry
        if not own:
            from_chip(j, 0).wait_recv()
        new_top = top
        biases = []
        for i in range(blocks):
            kb = (j * 2 + k) * blocks + i
            bias = jnp.zeros((1, both_rows), F32)
            for b in range(2 * blocks):
                live = lax.shift_right_logical(bits[b], kb) & 1
                bias = jnp.where(lane_block == b, jnp.where(live == 1, 0.0, -1e30), bias)
            part = pl.ds(i * TILE, TILE)
            s = mm(kv[j, 0, part], sq[...], 1, 1)
            if own:
                key = k * rows + i * TILE + lax.broadcasted_iota(jnp.int32, s.shape, 0)
                lane = lax.broadcasted_iota(jnp.int32, s.shape, 1)
                query = jnp.where(lane < rows, k * rows + lane, other * rows + lane - rows)
                s = jnp.where(key <= query, s, -1e30)
            sbuf[j, part] = s
            new_top = jnp.maximum(new_top, jnp.max(s, axis=0, keepdims=True) * factor + bias)
            biases.append(bias)
        alpha = jnp.exp2(top - new_top)
        total = total * alpha
        for i in range(blocks):
            part = pl.ds(i * TILE, TILE)
            e = jnp.exp2(sbuf[j, part] * factor + (biases[i] - new_top))
            sbuf[j, part] = e
            total = total + jnp.sum(e, axis=0, keepdims=True)
        tops[j] = new_top
        if not own:
            from_chip(j, 1).wait_recv()
        dpbuf[j] = mm(kv[j, 1], sdo[...], 1, 1)
        term = mm(kv[j, 1], sbuf[j].astype(BF), 0, 0)
        for i in range(2):
            lanes = slice(i * rows, (i + 1) * rows)
            if own:
                acc[i] = term[:, lanes]
            else:
                acc[i] = acc[i] * alpha[:, lanes] + term[:, lanes]
        return new_top, total

    swap_q.wait_recv()
    swap_do.wait_recv()
    carry = (jnp.full((1, both_rows), -3e30, F32), jnp.zeros((1, both_rows), F32))
    my_top, my_total = lax.fori_loop(
        1, p + 1, lambda step, carry: fold(p - step, carry, False), fold(p, carry, True)
    )

    stat[0:1] = my_top
    stat[1:2] = my_total
    stat[2:3] = jnp.concatenate(
        [
            jnp.sum(
                sdo[i * rows : (i + 1) * rows].astype(F32).T * acc[i], axis=0, keepdims=True
            )
            for i in range(2)
        ],
        axis=1,
    )
    swap_stat = rcopy(stat, stat_in, ps.at[2], pr.at[2], partner)
    swap_acc = rcopy(acc.at[1], acc_in, ps.at[3], pr.at[3], partner)
    swap_stat.start()
    swap_acc.start()

    @pl.loop(p + 1, chips)
    def _(j):
        for kk in range(2):
            state_send(j, 0, kk).start()

    def theirs(i):
        return jnp.concatenate([stat_in[i : i + 1, rows:], stat_in[i : i + 1, :rows]], axis=1)

    swap_stat.wait_recv()
    their_top = theirs(0)
    top = jnp.maximum(my_top, their_top)
    my_part_of = jnp.exp2(my_top - top)
    their_part_of = jnp.exp2(their_top - top)
    inv_total = 1.0 / (my_total * my_part_of + theirs(1) * their_part_of)
    delta = (stat[2:3] * my_part_of + theirs(2) * their_part_of) * inv_total

    def to_owner(t, j):
        return rcopy(
            g.at[t, j], rin.at[t, p], grs.at[t, j], grr.at[t, p], (j * 2 + k, h)
        )

    def value_term(j):
        prob = sbuf[j] * (jnp.exp2(tops[j] - top) * inv_total)
        return mm(prob.astype(BF), sdo[...], 1, 0)

    def key_term(j):
        ds = sbuf[j] * (jnp.exp2(tops[j] - top) * (inv_total * inv)) * (dpbuf[j] - delta)
        ds = ds.astype(BF)
        term = mm(kv[j, 0], ds, 0, 0)
        for i in range(2):
            dq[i] += term[:, i * rows : (i + 1) * rows]
        return mm(ds, sq[...], 1, 0)

    dq[...] = jnp.zeros_like(dq)

    far = chips - 1 - p

    def far_to_head(t, i):
        q = (h + i) % m
        return rcopy(fb.at[t, q], fbin.at[t, h], fzs.at[t, q], fzr.at[t, h], (c, q))

    def far_from_head(t, i):
        q = (h + i) % m
        return rcopy(fb.at[t, q], fbin.at[t, q], fzs.at[t, q], fzr.at[t, q], (c, q))

    def far_to_owner(t):
        return rcopy(fsum.at[t], fsum_in.at[t], fos.at[t], for_.at[t], (far * 2 + k, h))

    for t, term in ((1, value_term), (0, key_term)):
        if head_sum:

            @pl.when(far < p)
            def _(t=t, term=term):
                v = term(far).astype(BF)
                for q in range(m):
                    fb[t, q] = v[q * part_rows : (q + 1) * part_rows]
                for i in range(1, m):
                    far_to_head(t, i).start()

        @pl.loop(0, p)
        def _(j, t=t, term=term):
            @pl.when(jnp.logical_or(j != far, not head_sum))
            def _():
                g[t, j] = term(j).astype(BF)
                to_owner(t, j).start()

    g_own[1] = value_term(p)
    g_own[0] = key_term(p)
    swap_dq = rcopy(dq.at[1], dq_in, ps.at[4], pr.at[4], partner)
    swap_dq.start()

    swap_acc.wait_recv()
    out_t = (
        acc[0] * (my_part_of * inv_total)[:, :rows]
        + acc_in[...] * (their_part_of * inv_total)[:, :rows]
    )
    o[4] = out_t.T.astype(BF)

    if head_sum:

        @pl.when(far < p)
        def _():
            for t in (1, 0):
                total = fb[t, h].astype(F32)
                for i in range(1, m):
                    far_from_head(t, i).wait_recv()
                    total = total + fbin[t, (h + i) % m].astype(F32)
                fsum[t] = total.astype(BF)
                far_to_owner(t).start()

    kf = jnp.where(k == 1, 1.0, 0.0).astype(F32)
    prefix = st_par[0].astype(F32) * kf
    suffix = st_par[1].astype(F32) * (1.0 - kf)

    def add_state(j, v):
        for kk in range(2):
            state_recv(j, kk).wait_recv()
        return v + st_all[j].astype(F32)

    prefix = lax.fori_loop(0, p, add_state, prefix).astype(BF)
    suffix = lax.fori_loop(p + 1, chips, add_state, suffix).astype(BF)
    o[0] = (row_scale * (lin_acc[0] + mm(lq[...], prefix, 1, 0))).astype(BF)
    o[1] = (lin_acc[1] + mm(scot, prefix, 1, 1)).astype(BF)
    o[2] = (lin_acc[2] + mm(lv[...], suffix, 1, 1)).astype(BF)
    o[3] = (lin_acc[3] + mm(lk[...], suffix, 1, 0)).astype(BF)
    swap_dq.wait_recv()
    o[5] = (dq[0] + dq_in[...]).T.astype(BF)

    def owned(t):
        @pl.loop(p + 1, chips)
        def _(j):
            @pl.when(jnp.logical_or(j != far, not head_sum))
            def _():
                rcopy(g.at[t, j], rin.at[t, j], grs.at[t, j], grr.at[t, j], partner).wait_recv()
                g_own[t] += rin[t, j].astype(F32)

        return g_own[t]

    if head_sum:

        def to_head(t, i):
            q = (h + i) % m
            return rcopy(hb.at[t, q], hin.at[t, h], zs.at[t, q], zr.at[t, h], (c, q))

        def from_head(t, i):
            q = (h + i) % m
            return rcopy(hb.at[t, q], hin.at[t, q], zs.at[t, q], zr.at[t, q], (c, q))

        def result_to(t, i):
            q = (h + i) % m
            return rcopy(fq.at[t], fin.at[t, h], fs.at[t, q], fr.at[t, h], (c, q))

        def result_from(t, i):
            q = (h + i) % m
            return rcopy(fq.at[t], fin.at[t, q], fs.at[t, q], fr.at[t, q], (c, q))

        for t in (1, 0):
            mine = owned(t)
            for q in range(m):
                hb[t, q] = mine[q * part_rows : (q + 1) * part_rows].astype(BF)
            for i in range(1, m):
                to_head(t, i).start()
        for t in (1, 0):
            part = hb[t, h].astype(F32)
            for i in range(1, m):
                from_head(t, i).wait_recv()
                part = part + hin[t, (h + i) % m].astype(F32)
            psum[...] = part

            @pl.when(far > p)
            def _(t=t):
                far_to_owner(t).wait_recv()
                psum[...] += fsum_in[t].astype(F32)

            fq[t] = psum[...].astype(BF)
            for i in range(1, m):
                result_to(t, i).start()
            fin[t, h] = fq[t]
        for t in (1, 0):
            for i in range(1, m):
                result_from(t, i).wait_recv()
            for q in range(m):
                o[6 + t, q * part_rows : (q + 1) * part_rows] = fin[t, q]
            for i in range(1, m):
                to_head(t, i).wait_send()
                result_to(t, i).wait_send()

        @pl.when(far < p)
        def _():
            for t in range(2):
                for i in range(1, m):
                    far_to_head(t, i).wait_send()
                far_to_owner(t).wait_send()

    else:
        for t in (1, 0):
            o_sd[t] = owned(t)

    swap_q.wait_send()
    swap_do.wait_send()
    swap_stat.wait_send()
    swap_acc.wait_send()
    swap_dq.wait_send()

    @pl.loop(0, p)
    def _(j):
        for kk in range(2):
            state_send(j, 1, kk).wait_send()

        @pl.when(jnp.logical_or(j != far, not head_sum))
        def _():
            for t in range(2):
                to_owner(t, j).wait_send()

    @pl.loop(p + 1, chips)
    def _(j):
        for t in range(2):
            to_chip(j, t).wait_send()
        for kk in range(2):
            state_send(j, 0, kk).wait_send()


def body(n, m, lin_q, lin_k, lin_v, lin_do, soft_q, soft_k, soft_v, soft_do, tile_list, tile_count):
    rows, d = lin_q.shape
    chips = n // 2
    head_sum = rows % (16 * m) == 0
    vmem = pl.BlockSpec(memory_space=pltpu.VMEM)
    hbm = pl.BlockSpec(memory_space=pltpu.HBM)
    if head_sum:
        out_shape = (pltpu.VMEM((8, rows, d), BF),)
    else:
        out_shape = (pltpu.VMEM((6, rows, d), BF), pltpu.VMEM((2, rows, d), F32))
    args = [
        pltpu.with_memory_space_constraint(x, pltpu.HBM)
        for x in (
            lin_q, lin_k, lin_v, lin_do, soft_q, soft_k, soft_v, soft_do, tile_list, tile_count
        )
    ]
    one = pltpu.VMEM((rows, d), BF)
    pair = pltpu.VMEM((2 * rows, d), BF)
    pr = rows // m if head_sum else 16
    dma = pltpu.SemaphoreType.DMA
    outs = pl.pallas_call(
        functools.partial(layer_kernel, n, m, head_sum),
        name="layer",
        out_shape=out_shape,
        in_specs=[hbm] * 10,
        out_specs=(vmem,) * len(out_shape),
        scratch_shapes=[
            one, one, one, one, pair, pair,
            pltpu.SMEM(tile_list.shape, jnp.int32),
            pltpu.SMEM(tile_count.shape, jnp.int32),
            pltpu.VMEM((chips, 2, rows, d), BF),
            pltpu.VMEM((chips, rows, 2 * rows), F32),
            pltpu.VMEM((chips, rows, 2 * rows), F32),
            pltpu.VMEM((2, d, d), BF),
            pltpu.VMEM((2, d, d), BF),
            pltpu.VMEM((2, d, d), BF),
            pltpu.VMEM((chips, d, d), BF),
            pltpu.VMEM((4, rows, d), F32),
            pltpu.VMEM((2, chips, rows, d), BF),
            pltpu.VMEM((2, chips, rows, d), BF),
            pltpu.VMEM((2, d, rows), F32),
            pltpu.VMEM((d, rows), F32),
            pltpu.VMEM((2, d, rows), F32),
            pltpu.VMEM((d, rows), F32),
            pltpu.VMEM((8, 2 * rows), F32),
            pltpu.VMEM((8, 2 * rows), F32),
            pltpu.VMEM((2, rows, d), F32),
            pltpu.VMEM((2, m, pr, d), BF),
            pltpu.VMEM((2, m, pr, d), BF),
            pltpu.VMEM((2, pr, d), BF),
            pltpu.VMEM((2, m, pr, d), BF),
            pltpu.VMEM((2, m, pr, d), BF),
            pltpu.VMEM((2, m, pr, d), BF),
            pltpu.VMEM((2, pr, d), BF),
            pltpu.VMEM((2, pr, d), BF),
            pltpu.VMEM((pr, d), F32),
            pltpu.VMEM((chips, 1, 2 * rows), F32),
            dma((10,)),
            dma((chips, 2)), dma((chips, 2)), dma((5,)), dma((5,)),
            dma, dma,
            dma((chips, 2)), dma((chips, 2)),
            dma((2, chips)), dma((2, chips)),
            dma((2, m)), dma((2, m)), dma((2, m)), dma((2, m)),
            dma((2, m)), dma((2, m)), dma((2,)), dma((2,)),
        ],
        compiler_params=pltpu.CompilerParams(
            collective_id=0, has_side_effects=True, vmem_limit_bytes=40 << 20
        ),
    )(*args)
    if head_sum:
        return tuple(outs[0][i] for i in range(8))
    soft_d = lax.psum(outs[1], "head").astype(BF)
    return tuple(outs[0][i] for i in range(6)) + (soft_d[0], soft_d[1])


def solution(mesh):
    n, m = mesh.shape["ctx"], mesh.shape["head"]
    both = P("ctx", "head")
    seq = P("ctx", None)
    return jax.shard_map(
        functools.partial(body, n, m),
        mesh=mesh,
        in_specs=(both, both, both, both, both, seq, seq, both, P(), P()),
        out_specs=(both,) * 6 + (seq, seq),
        check_vma=False,
    )
```

```python
import functools
import math

import jax
import jax.numpy as jnp
from jax import lax
from jax.experimental import pallas as pl
from jax.experimental.pallas import tpu as pltpu
from jax.sharding import PartitionSpec as P

TILE = 128
BF = jnp.bfloat16
F32 = jnp.float32
MESH = pl.DeviceIdType.MESH


def mm(a, b, da, db):
    return lax.dot_general(a, b, (((da,), (db,)), ((), ())), preferred_element_type=F32)


def layer_kernel(
    n, m, head_sum,
    lq_in, lk_in, lv_in, ldo_in, sq_in, sk_in, sv_in, sdo_in, tl_in, tc_in,
    *refs,
):
    if head_sum:
        o, *refs = refs
    else:
        o, o_sd, *refs = refs
    (
        lq, lk, lv, ldo, sq, sdo, tl, tc, kv, sbuf, dpbuf, dsb, do_t, st_own, st_par, st_half,
        st_all, lin_acc, g, rin, acc, dq, core_in, side_out, side_in, stat, stat_in, g_own,
        fq, fin, tops, ins,
        kvs, kvr, qs, qr, es, er, ws, wr, xs, xr, hs, hr, grs, grr, fs, fr,
    ) = refs
    rows, d = lq.shape
    chips = n // 2
    c = lax.axis_index("ctx")
    h = lax.axis_index("head")
    p = c // 2
    k = c % 2
    other = 1 - k
    side = h % 2
    h2 = h + 1 - 2 * side
    partner = (p * 2 + other, h)
    neighbour = (c, h2)
    diagonal = (p * 2 + other, h2)
    key_rows = rows // 2
    half = pl.ds(pl.multiple_of(side * key_rows, key_rows), key_rows)
    first = pl.ds(0, rows)
    second = pl.ds(rows, rows)
    loads = []
    for i, (a, b) in enumerate((
        (sk_in.at[half], kv.at[p, 0]), (sv_in.at[half], kv.at[p, 1]),
        (sq_in, sq.at[0, first]), (sdo_in, sdo.at[0, first]),
        (lk_in, lk), (lv_in, lv), (lq_in, lq), (ldo_in, ldo), (tl_in, tl), (tc_in, tc),
    )):
        loads.append(pltpu.make_async_copy(a, b, ins.at[i]))
    inv = 1.0 / math.sqrt(d)

    def rcopy(src, dst, s, r, dev):
        return pltpu.make_async_remote_copy(
            src_ref=src, dst_ref=dst, send_sem=s, recv_sem=r, device_id=dev, device_id_type=MESH
        )

    for load in loads:
        load.start()
    barrier = pltpu.get_barrier_semaphore()
    greet = [((c + i) % n, h) for i in range(1, n)] + [diagonal]
    groups = m // 2 if head_sum else 1
    group = h // 2 if head_sum else 0
    greet += [(c, (h + i) % m) for i in range(1, m)] if head_sum else [neighbour]
    greet += [
        ((p + i) % chips * 2 + k, (group + q) % groups * 2 + side)
        for i in range(1, chips)
        for q in range(1, groups)
    ]
    for device in greet:
        pl.semaphore_signal(barrier, inc=1, device_id=device, device_id_type=MESH)

    for load in loads[4:8]:
        load.wait()
    pos = (c * rows + lax.broadcasted_iota(jnp.int32, (rows, d), 0) + 1).astype(F32)
    row_scale = 1.0 / jnp.sqrt(d * pos)
    scot = (ldo[...].astype(F32) * row_scale).astype(BF)
    st_own[0] = mm(lk[...], lv[...], 0, 0).astype(BF)
    st_own[1] = mm(lq[...], scot, 0, 0).astype(BF)
    for load in loads[:4] + loads[8:]:
        load.wait()
    blocks = rows // TILE
    bits = []
    for seg in (c, p * 2 + other):
        for b in range(blocks):
            row = seg * blocks + b
            word = jnp.int32(0)
            for s in range(tl.shape[1]):
                bit = lax.shift_left(jnp.int32(1), tl[row, s])
                word = word | jnp.where(s < tc[row], bit, 0)
            bits.append(word)
    pl.semaphore_wait(barrier, len(greet))

    def to_chip(j, t):
        return rcopy(kv.at[p, t], kv.at[p, t], kvs.at[j, t], kvr.at[p, t], (j * 2 + k, h))

    def from_chip(j, t):
        return rcopy(kv.at[p, t], kv.at[j, t], kvs.at[j, t], kvr.at[j, t], (j * 2 + k, h))

    def query_copies(buf, t):
        return (
            rcopy(buf.at[0, first], buf.at[1, first], qs.at[t, 0], qr.at[t, 0], neighbour),
            rcopy(buf.at[0, first], buf.at[0, second], qs.at[t, 1], qr.at[t, 1], partner),
            rcopy(buf.at[1, first], buf.at[1, second], qs.at[t, 2], qr.at[t, 2], partner),
        )

    swaps = (query_copies(sq, 0), query_copies(sdo, 1))
    swaps[0][0].start()

    @pl.loop(p + 1, chips)
    def _(i):
        j = chips - (i - p)
        to_chip(j, 0).start()
        to_chip(j, 1).start()

    swaps[0][1].start()
    swaps[1][1].start()
    exchange = rcopy(st_own, st_par, xs, xr, partner)
    exchange.start()

    tri = lax.broadcasted_iota(jnp.int32, (rows, rows), 0) >= lax.broadcasted_iota(
        jnp.int32, (rows, rows), 1
    )
    aqk = jnp.where(tri, mm(lq[...], lk[...], 1, 1), 0.0).astype(BF)
    adv = jnp.where(tri, mm(scot, lv[...], 1, 1), 0.0).astype(BF)
    lin_acc[0] = mm(aqk, lv[...], 1, 0)
    lin_acc[1] = mm(adv, lk[...], 1, 0)
    lin_acc[2] = mm(adv, lq[...], 0, 0)
    lin_acc[3] = mm(aqk, scot, 0, 0)
    swaps[1][0].start()

    exchange.wait()
    st_half[...] = (st_own[...].astype(F32) + st_par[...].astype(F32)).astype(BF)
    hd = d // 2
    my_part = pl.ds(pl.multiple_of(k * hd, hd), hd)

    def state_send(j, t, kk):
        return rcopy(
            st_half.at[t, my_part], st_all.at[p, my_part], hs.at[j, kk], hr.at[p, k],
            (j * 2 + kk, h),
        )

    def state_recv(j, kk):
        part = pl.ds(kk * hd, hd)
        return rcopy(
            st_half.at[0, part], st_all.at[j, part], hs.at[j, kk], hr.at[j, kk], partner
        )

    @pl.loop(0, p)
    def _(j):
        for kk in range(2):
            state_send(j, 1, kk).start()

    both_rows = 2 * rows
    key_blocks = key_rows // TILE
    lane_block = lax.broadcasted_iota(jnp.int32, (1, both_rows), 1) // TILE
    factor = inv * math.log2(math.e)

    def fold(j, u, carry, own, wait):
        top, total = carry
        if wait:
            from_chip(j, 0).wait_recv()
        biases = []
        for i in range(key_blocks):
            kb = (j * 2 + k) * blocks + side * key_blocks + i
            bias = jnp.zeros((1, both_rows), F32)
            for b in range(2 * blocks):
                live = lax.shift_right_logical(bits[b], kb) & 1
                bias = jnp.where(lane_block == b, jnp.where(live == 1, 0.0, -1e30), bias)
            biases.append(bias)
        new_top = top
        for i in range(key_blocks):
            part = pl.ds(i * TILE, TILE)
            s = mm(kv[j, 0, part], sq[u], 1, 1)
            if own:
                key = (
                    k * rows + side * key_rows + i * TILE
                    + lax.broadcasted_iota(jnp.int32, s.shape, 0)
                )
                lane = lax.broadcasted_iota(jnp.int32, s.shape, 1)
                query = jnp.where(lane < rows, k * rows + lane, other * rows + lane - rows)
                s = jnp.where(key <= query, s, -1e30)
            sbuf[j, u, part] = s
            top_here = jnp.max(s, axis=0, keepdims=True) * factor + biases[i]
            new_top = jnp.maximum(new_top, top_here)
        alpha = jnp.exp2(top - new_top)
        total = total * alpha
        for i in range(key_blocks):
            part = pl.ds(i * TILE, TILE)
            e = jnp.exp2(sbuf[j, u, part] * factor + (biases[i] - new_top))
            sbuf[j, u, part] = e
            total = total + jnp.sum(e, axis=0, keepdims=True)
        tops[j, u] = new_top
        if wait:
            from_chip(j, 1).wait_recv()
        term = mm(kv[j, 1], sbuf[j, u].astype(BF), 0, 0)
        for i in range(2):
            lanes = slice(i * rows, (i + 1) * rows)
            if own:
                acc[2 * u + i] = term[:, lanes]
            else:
                acc[2 * u + i] = acc[2 * u + i] * alpha[:, lanes] + term[:, lanes]
        return new_top, total

    empty = (jnp.full((1, both_rows), -3e30, F32), jnp.zeros((1, both_rows), F32))
    near = jnp.minimum(p, 1) + 1
    swaps[0][1].wait_recv()
    mine = fold(p, 0, empty, True, False)
    swaps[0][0].wait_recv()
    swaps[0][2].start()
    mine = lax.fori_loop(1, near, lambda i, v: fold(p - i, 0, v, False, True), mine)
    swaps[1][0].wait_recv()
    swaps[1][2].start()
    swaps[0][2].wait_recv()
    side_carry = fold(p, 1, empty, True, False)
    side_carry = lax.fori_loop(
        1, near, lambda i, v: fold(p - i, 1, v, False, False), side_carry
    )

    def fold_both(i, v):
        return fold(p - i, 0, v[:2], False, True) + fold(p - i, 1, v[2:], False, False)

    carry = lax.fori_loop(near, p + 1, fold_both, mine + side_carry)
    swaps[1][1].wait_recv()
    swaps[1][2].wait_recv()
    for u in range(2):
        for i in range(2):
            do_t[2 * u + i] = sdo[u, i * rows : (i + 1) * rows].astype(F32).T

    my_top = jnp.concatenate([carry[0], carry[2]], axis=1)
    my_total = jnp.concatenate([carry[1], carry[3]], axis=1)
    my_delta = jnp.concatenate(
        [jnp.sum(do_t[i] * acc[i], axis=0, keepdims=True) for i in range(4)], axis=1
    )
    stat[0] = my_top
    stat[1] = my_total
    stat[2] = my_delta
    stats = [
        rcopy(stat, stat_in.at[i], es.at[i], er.at[i], device)
        for i, device in enumerate((partner, neighbour, diagonal))
    ]
    for i in (1, 2, 0):
        stats[i].start()

    def to_core(t, i):
        src = (acc, dq)[t]
        return rcopy(src.at[2 * i + 1], core_in.at[t, i], ws.at[t, i], wr.at[t, i], partner)

    def to_side(t):
        return rcopy(side_out.at[t], side_in.at[t], ws.at[t, 2], wr.at[t, 2], neighbour)

    for i in (1, 0):
        to_core(0, i).start()

    @pl.loop(p + 1, chips)
    def _(j):
        for kk in range(2):
            state_send(j, 0, kk).start()

    @pl.loop(0, p + 1)
    def _(j):
        for u in range(2):
            dpbuf[j, u] = mm(kv[j, 1], sdo[u], 1, 1)

    for swap in stats:
        swap.wait_recv()

    def theirs(i, row):
        return jnp.concatenate(
            [
                stat_in[i, row, :, (x ^ (i + 1)) * rows : ((x ^ (i + 1)) + 1) * rows]
                for x in range(4)
            ],
            axis=1,
        )

    top = my_top
    for i in range(3):
        top = jnp.maximum(top, theirs(i, 0))
    my_part_of = jnp.exp2(my_top - top)
    total = my_total * my_part_of
    delta = my_delta * my_part_of
    for i in range(3):
        their_part_of = jnp.exp2(theirs(i, 0) - top)
        total = total + theirs(i, 1) * their_part_of
        delta = delta + theirs(i, 2) * their_part_of
    inv_total = 1.0 / total
    delta = delta * inv_total

    weight = my_part_of * inv_total
    core_weight = jnp.exp2(theirs(0, 0) - top) * inv_total

    def slot_out(x):
        lanes = slice(x * rows, (x + 1) * rows)
        return acc[x] * weight[:, lanes] + core_in[0, x // 2] * core_weight[:, lanes]

    to_core(0, 1).wait_recv()
    side_out[0] = slot_out(2).astype(BF)
    to_side(0).start()

    def halves(v):
        return v[:, :both_rows], v[:, both_rows:]

    tops_final, inv_totals, deltas = halves(top), halves(inv_total), halves(delta)

    piece = key_rows // groups

    def to_owner(t, j, i):
        q = (group + i) % groups
        return rcopy(
            g.at[t, j, q], rin.at[t, p, group], grs.at[t, j, q], grr.at[t, p, group],
            (j * 2 + k, q * 2 + side if head_sum else h),
        )

    def from_owner(t, j, i):
        q = (group + i) % groups
        return rcopy(
            g.at[t, j, q], rin.at[t, j, q], grs.at[t, j, q], grr.at[t, j, q], partner
        )

    def put(t, j, v):
        for q in range(groups):
            g[t, j, q] = v[q * piece : (q + 1) * piece].astype(BF)

    def value_term(j):
        v = 0.0
        for u in range(2):
            prob = sbuf[j, u] * (jnp.exp2(tops[j, u] - tops_final[u]) * inv_totals[u])
            v = v + mm(prob.astype(BF), sdo[u], 1, 0)
        return v

    def key_term(j):
        v = 0.0
        for u in range(2):
            scale = jnp.exp2(tops[j, u] - tops_final[u]) * (inv_totals[u] * inv)
            ds = (sbuf[j, u] * scale * (dpbuf[j, u] - deltas[u])).astype(BF)
            dsb[u] = ds
            v = v + mm(ds, sq[u], 1, 0)
        return v

    def query_term(j):
        for u in range(2):
            term = mm(kv[j, 0], dsb[u], 0, 0)
            for i in range(2):
                dq[2 * u + i] += term[:, i * rows : (i + 1) * rows]

    dq[...] = jnp.zeros_like(dq)

    terms = ((1, value_term), (0, key_term))

    @pl.loop(0, p)
    def _(j):
        for t, term in terms:
            put(t, j, term(j))
            for i in range(groups - 1, -1, -1):
                to_owner(t, j, i).start()
        query_term(j)

    for t, term in terms:
        mine = term(p)
        for q in range(groups):
            g_own[t, q] = mine[q * piece : (q + 1) * piece]
        put(t, p, mine)
        for i in range(1, groups):
            to_owner(t, p, i).start()
    query_term(p)

    for i in (1, 0):
        to_core(1, i).start()

    def owned(t):
        total = g_own[t, group]
        for i in range(1, groups):
            from_owner(t, p, i).wait_recv()
            total = total + rin[t, p, (group + i) % groups].astype(F32)

        def add_grad(j, v):
            for i in range(groups):
                from_owner(t, j, i).wait_recv()
                v = v + rin[t, j, (group + i) % groups].astype(F32)
            return v

        return lax.fori_loop(p + 1, chips, add_grad, total)

    to_core(1, 1).wait_recv()
    side_out[1] = (dq[2] + core_in[1, 1]).astype(BF)
    to_side(1).start()

    kf = jnp.where(k == 1, 1.0, 0.0).astype(F32)
    prefix = st_par[0].astype(F32) * kf
    suffix = st_par[1].astype(F32) * (1.0 - kf)

    def add_state(j, v):
        for kk in range(2):
            state_recv(j, kk).wait_recv()
        return v + st_all[j].astype(F32)

    prefix = lax.fori_loop(0, p, add_state, prefix).astype(BF)
    suffix = lax.fori_loop(p + 1, chips, add_state, suffix).astype(BF)
    o[0] = (row_scale * (lin_acc[0] + mm(lq[...], prefix, 1, 0))).astype(BF)
    o[1] = (lin_acc[1] + mm(scot, prefix, 1, 1)).astype(BF)
    o[2] = (lin_acc[2] + mm(lv[...], suffix, 1, 1)).astype(BF)
    o[3] = (lin_acc[3] + mm(lk[...], suffix, 1, 0)).astype(BF)

    def finish(t):
        to_core(t, 0).wait_recv()
        to_side(t).wait_recv()
        out = dq[0] + core_in[1, 0] if t else slot_out(0)
        o[4 + t] = (out + side_in[t].astype(F32)).T.astype(BF)

    if head_sum:

        def result_to(t, i):
            q = (h + i) % m
            return rcopy(fq.at[t], fin.at[t, h], fs.at[t, q], fr.at[t, h], (c, q))

        def result_from(t, i):
            q = (h + i) % m
            return rcopy(fq.at[t], fin.at[t, q], fs.at[t, q], fr.at[t, q], (c, q))

        for t in (1, 0):
            fq[t] = owned(t).astype(BF)
            for i in range(1, m):
                result_to(t, i).start()
            fin[t, h] = fq[t]
        for t in range(2):
            finish(t)
        for t in (1, 0):
            for i in range(1, m):
                result_from(t, i).wait_recv()
            for q in range(m):
                start = (q % 2) * key_rows + (q // 2) * piece
                o[6 + t, start : start + piece] = fin[t, q]
        for t in (1, 0):
            for i in range(1, groups):
                to_owner(t, p, i).wait_send()
            for i in range(1, m):
                result_to(t, i).wait_send()
    else:
        o_sd[...] = jnp.zeros_like(o_sd)
        for t in (1, 0):
            o_sd[t, half] = owned(t)
        for t in range(2):
            finish(t)

    for t in range(2):
        for swap in swaps[t]:
            swap.wait_send()
        for i in range(2):
            to_core(t, i).wait_send()
        to_side(t).wait_send()
    for swap in stats:
        swap.wait_send()

    @pl.loop(0, p)
    def _(j):
        for kk in range(2):
            state_send(j, 1, kk).wait_send()
        for t in range(2):
            for i in range(groups):
                to_owner(t, j, i).wait_send()

    @pl.loop(p + 1, chips)
    def _(j):
        for t in range(2):
            to_chip(j, t).wait_send()
        for kk in range(2):
            state_send(j, 0, kk).wait_send()


def body(n, m, lin_q, lin_k, lin_v, lin_do, soft_q, soft_k, soft_v, soft_do, tile_list, tile_count):
    rows, d = lin_q.shape
    chips = n // 2
    head_sum = rows % (16 * m) == 0
    vmem = pl.BlockSpec(memory_space=pltpu.VMEM)
    hbm = pl.BlockSpec(memory_space=pltpu.HBM)
    if head_sum:
        out_shape = (pltpu.VMEM((8, rows, d), BF),)
    else:
        out_shape = (pltpu.VMEM((6, rows, d), BF), pltpu.VMEM((2, rows, d), F32))
    args = [
        pltpu.with_memory_space_constraint(x, pltpu.HBM)
        for x in (
            lin_q, lin_k, lin_v, lin_do, soft_q, soft_k, soft_v, soft_do, tile_list, tile_count
        )
    ]
    one = pltpu.VMEM((rows, d), BF)
    pair = pltpu.VMEM((2, 2 * rows, d), BF)
    kr = rows // 2
    groups = m // 2 if head_sum else 1
    pr = rows // m if head_sum else 16
    dma = pltpu.SemaphoreType.DMA
    outs = pl.pallas_call(
        functools.partial(layer_kernel, n, m, head_sum),
        name="layer",
        out_shape=out_shape,
        in_specs=[hbm] * 10,
        out_specs=(vmem,) * len(out_shape),
        scratch_shapes=[
            one, one, one, one, pair, pair,
            pltpu.SMEM(tile_list.shape, jnp.int32),
            pltpu.SMEM(tile_count.shape, jnp.int32),
            pltpu.VMEM((chips, 2, kr, d), BF),
            pltpu.VMEM((chips, 2, kr, 2 * rows), F32),
            pltpu.VMEM((chips, 2, kr, 2 * rows), F32),
            pltpu.VMEM((2, kr, 2 * rows), BF),
            pltpu.VMEM((4, d, rows), F32),
            pltpu.VMEM((2, d, d), BF),
            pltpu.VMEM((2, d, d), BF),
            pltpu.VMEM((2, d, d), BF),
            pltpu.VMEM((chips, d, d), BF),
            pltpu.VMEM((4, rows, d), F32),
            pltpu.VMEM((2, chips, groups, kr // groups, d), BF),
            pltpu.VMEM((2, chips, groups, kr // groups, d), BF),
            pltpu.VMEM((4, d, rows), F32),
            pltpu.VMEM((4, d, rows), F32),
            pltpu.VMEM((2, 2, d, rows), F32),
            pltpu.VMEM((2, d, rows), BF),
            pltpu.VMEM((2, d, rows), BF),
            pltpu.VMEM((3, 1, 4 * rows), F32),
            pltpu.VMEM((3, 3, 1, 4 * rows), F32),
            pltpu.VMEM((2, groups, kr // groups, d), F32),
            pltpu.VMEM((2, pr, d), BF),
            pltpu.VMEM((2, m, pr, d), BF),
            pltpu.VMEM((chips, 2, 1, 2 * rows), F32),
            dma((10,)),
            dma((chips, 2)), dma((chips, 2)), dma((2, 3)), dma((2, 3)),
            dma((3,)), dma((3,)), dma((2, 3)), dma((2, 3)),
            dma, dma,
            dma((chips, 2)), dma((chips, 2)),
            dma((2, chips, groups)), dma((2, chips, groups)), dma((2, m)), dma((2, m)),
        ],
        compiler_params=pltpu.CompilerParams(
            collective_id=0, has_side_effects=True, vmem_limit_bytes=40 << 20
        ),
    )(*args)
    if head_sum:
        return tuple(outs[0][i] for i in range(8))
    soft_d = lax.psum(outs[1], "head").astype(BF)
    return tuple(outs[0][i] for i in range(6)) + (soft_d[0], soft_d[1])


def solution(mesh):
    n, m = mesh.shape["ctx"], mesh.shape["head"]
    both = P("ctx", "head")
    seq = P("ctx", None)
    return jax.shard_map(
        functools.partial(body, n, m),
        mesh=mesh,
        in_specs=(both, both, both, both, both, seq, seq, both, P(), P()),
        out_specs=(both,) * 6 + (seq, seq),
        check_vma=False,
    )
```

```python
import functools
import math

import jax
import jax.numpy as jnp
from jax import lax
from jax.experimental import pallas as pl
from jax.experimental.pallas import tpu as pltpu
from jax.sharding import PartitionSpec as P

TILE = 128
BF = jnp.bfloat16
F32 = jnp.float32
MESH = pl.DeviceIdType.MESH


def mm(a, b, da, db):
    return lax.dot_general(a, b, (((da,), (db,)), ((), ())), preferred_element_type=F32)


def layer_kernel(
    n, m, head_sum,
    lq_in, lk_in, lv_in, ldo_in, sq_in, sk_in, sv_in, sdo_in, tl_in, tc_in,
    *refs,
):
    if head_sum:
        o, *refs = refs
    else:
        o, o_sd, *refs = refs
    (
        lq, lk, lv, ldo, sq, sdo, tl, tc, kv, sbuf, dpbuf, dsb, ebuf, do_t, st_own, st_par, st_half,
        st_all, lin_acc, g, rin, acc, dq, core_in, side_out, side_in, stat, stat_in, g_own,
        fq, fin, tops, ins,
        kvs, kvr, qs, qr, es, er, ws, wr, xs, xr, hs, hr, grs, grr, fs, fr,
    ) = refs
    rows, d = lq.shape
    chips = n // 2
    c = lax.axis_index("ctx")
    h = lax.axis_index("head")
    p = c // 2
    k = c % 2
    other = 1 - k
    side = h % 2
    h2 = h + 1 - 2 * side
    partner = (p * 2 + other, h)
    neighbour = (c, h2)
    diagonal = (p * 2 + other, h2)
    key_rows = rows // 2
    half = pl.ds(pl.multiple_of(side * key_rows, key_rows), key_rows)
    first = pl.ds(0, rows)
    second = pl.ds(rows, rows)
    loads = []
    for i, (a, b) in enumerate((
        (sk_in.at[half], kv.at[p, 0]), (sv_in.at[half], kv.at[p, 1]),
        (sq_in, sq.at[0, first]), (sdo_in, sdo.at[0, first]),
        (lk_in, lk), (lv_in, lv), (lq_in, lq), (ldo_in, ldo), (tl_in, tl), (tc_in, tc),
    )):
        loads.append(pltpu.make_async_copy(a, b, ins.at[i]))
    inv = 1.0 / math.sqrt(d)

    def rcopy(src, dst, s, r, dev):
        return pltpu.make_async_remote_copy(
            src_ref=src, dst_ref=dst, send_sem=s, recv_sem=r, device_id=dev, device_id_type=MESH
        )

    for load in loads:
        load.start()
    barrier = pltpu.get_barrier_semaphore()
    greet = [((c + i) % n, h) for i in range(1, n)] + [diagonal]
    groups = m // 2 if head_sum else 1
    group = h // 2 if head_sum else 0
    greet += [(c, (h + i) % m) for i in range(1, m)] if head_sum else [neighbour]
    greet += [
        ((p + i) % chips * 2 + k, (group + q) % groups * 2 + side)
        for i in range(1, chips)
        for q in range(1, groups)
    ]
    for device in greet:
        pl.semaphore_signal(barrier, inc=1, device_id=device, device_id_type=MESH)

    for load in loads[4:8]:
        load.wait()
    pos = (c * rows + lax.broadcasted_iota(jnp.int32, (rows, d), 0) + 1).astype(F32)
    row_scale = 1.0 / jnp.sqrt(d * pos)
    scot = (ldo[...].astype(F32) * row_scale).astype(BF)
    st_own[0] = mm(lk[...], lv[...], 0, 0).astype(BF)
    st_own[1] = mm(lq[...], scot, 0, 0).astype(BF)
    for load in loads[:4] + loads[8:]:
        load.wait()
    blocks = rows // TILE
    bits = []
    for seg in (c, p * 2 + other):
        for b in range(blocks):
            row = seg * blocks + b
            word = jnp.int32(0)
            for s in range(tl.shape[1]):
                bit = lax.shift_left(jnp.int32(1), tl[row, s])
                word = word | jnp.where(s < tc[row], bit, 0)
            bits.append(word)
    pl.semaphore_wait(barrier, len(greet))

    def to_chip(j, t):
        return rcopy(kv.at[p, t], kv.at[p, t], kvs.at[j, t], kvr.at[p, t], (j * 2 + k, h))

    def from_chip(j, t):
        return rcopy(kv.at[p, t], kv.at[j, t], kvs.at[j, t], kvr.at[j, t], (j * 2 + k, h))

    def query_copies(buf, t):
        return (
            rcopy(buf.at[0, first], buf.at[1, first], qs.at[t, 0], qr.at[t, 0], neighbour),
            rcopy(buf.at[0, first], buf.at[0, second], qs.at[t, 1], qr.at[t, 1], partner),
            rcopy(buf.at[1, first], buf.at[1, second], qs.at[t, 2], qr.at[t, 2], partner),
        )

    swaps = (query_copies(sq, 0), query_copies(sdo, 1))
    swaps[0][0].start()

    @pl.loop(p + 1, chips)
    def _(i):
        j = chips - (i - p)
        to_chip(j, 0).start()
        to_chip(j, 1).start()

    swaps[0][1].start()
    swaps[1][1].start()
    exchange = rcopy(st_own, st_par, xs, xr, partner)
    exchange.start()

    tri = lax.broadcasted_iota(jnp.int32, (rows, rows), 0) >= lax.broadcasted_iota(
        jnp.int32, (rows, rows), 1
    )
    aqk = jnp.where(tri, mm(lq[...], lk[...], 1, 1), 0.0).astype(BF)
    adv = jnp.where(tri, mm(scot, lv[...], 1, 1), 0.0).astype(BF)
    lin_acc[0] = mm(aqk, lv[...], 1, 0)
    lin_acc[1] = mm(adv, lk[...], 1, 0)
    lin_acc[2] = mm(adv, lq[...], 0, 0)
    lin_acc[3] = mm(aqk, scot, 0, 0)
    swaps[1][0].start()

    exchange.wait()
    st_half[...] = (st_own[...].astype(F32) + st_par[...].astype(F32)).astype(BF)
    hd = d // 2
    my_part = pl.ds(pl.multiple_of(k * hd, hd), hd)

    def state_send(j, t, kk):
        return rcopy(
            st_half.at[t, my_part], st_all.at[p, my_part], hs.at[j, kk], hr.at[p, k],
            (j * 2 + kk, h),
        )

    def state_recv(j, kk):
        part = pl.ds(kk * hd, hd)
        return rcopy(
            st_half.at[0, part], st_all.at[j, part], hs.at[j, kk], hr.at[j, kk], partner
        )

    @pl.loop(0, p)
    def _(j):
        for kk in range(2):
            state_send(j, 1, kk).start()

    both_rows = 2 * rows
    key_blocks = key_rows // TILE
    lane_block = lax.broadcasted_iota(jnp.int32, (1, both_rows), 1) // TILE
    factor = inv * math.log2(math.e)

    def fold(j, sides, carry, own, wait):
        if wait:
            from_chip(j, 0).wait_recv()
        biases = []
        for i in range(key_blocks):
            kb = (j * 2 + k) * blocks + side * key_blocks + i
            bias = jnp.zeros((1, both_rows), F32)
            for b in range(2 * blocks):
                live = lax.shift_right_logical(bits[b], kb) & 1
                bias = jnp.where(lane_block == b, jnp.where(live == 1, 0.0, -1e30), bias)
            biases.append(bias)
        tops_here, totals = list(carry[0::2]), list(carry[1::2])
        alphas = []
        for x, u in enumerate(sides):
            new_top = tops_here[x]
            for i in range(key_blocks):
                part = pl.ds(i * TILE, TILE)
                s = mm(kv[j, 0, part], sq[u], 1, 1)
                if own:
                    key = (
                        k * rows + side * key_rows + i * TILE
                        + lax.broadcasted_iota(jnp.int32, s.shape, 0)
                    )
                    lane = lax.broadcasted_iota(jnp.int32, s.shape, 1)
                    query = jnp.where(lane < rows, k * rows + lane, other * rows + lane - rows)
                    s = jnp.where(key <= query, s, -1e30)
                sbuf[j, u, part] = s
                top_here = jnp.max(s, axis=0, keepdims=True) * factor + biases[i]
                new_top = jnp.maximum(new_top, top_here)
            alphas.append(jnp.exp2(tops_here[x] - new_top))
            tops_here[x] = new_top
            tops[j, u] = new_top
        if wait:
            from_chip(j, 1).wait_recv()
        for x, u in enumerate(sides):
            total = totals[x] * alphas[x]
            for i in range(key_blocks):
                part = pl.ds(i * TILE, TILE)
                e = jnp.exp2(sbuf[j, u, part] * factor + (biases[i] - tops_here[x]))
                sbuf[j, u, part] = e
                ebuf[u, part] = e.astype(BF)
                total = total + jnp.sum(e, axis=0, keepdims=True)
            totals[x] = total
            term = mm(kv[j, 1], ebuf[u], 0, 0)
            for i in range(2):
                lanes = slice(i * rows, (i + 1) * rows)
                if own:
                    acc[2 * u + i] = term[:, lanes]
                else:
                    acc[2 * u + i] = acc[2 * u + i] * alphas[x][:, lanes] + term[:, lanes]
        return tuple(v for pair in zip(tops_here, totals) for v in pair)

    def transpose_cot(u):
        for i in range(2):
            do_t[2 * u + i] = sdo[u, i * rows : (i + 1) * rows].astype(F32).T

    empty = (jnp.full((1, both_rows), -3e30, F32), jnp.zeros((1, both_rows), F32))
    near = jnp.minimum(p, 1) + 1
    swaps[0][1].wait_recv()
    mine = fold(p, (0,), empty, True, False)
    swaps[1][1].wait_recv()
    transpose_cot(0)
    swaps[0][0].wait_recv()
    swaps[0][2].start()
    mine = lax.fori_loop(1, near, lambda i, v: fold(p - i, (0,), v, False, True), mine)
    swaps[1][0].wait_recv()
    swaps[1][2].start()
    swaps[0][2].wait_recv()
    side_carry = fold(p, (1,), empty, True, False)
    side_carry = lax.fori_loop(
        1, near, lambda i, v: fold(p - i, (1,), v, False, False), side_carry
    )

    def fold_both(i, v):
        return fold(p - i, (0, 1), v, False, True)

    carry = lax.fori_loop(near, p + 1, fold_both, mine + side_carry)
    my_top = jnp.concatenate([carry[0], carry[2]], axis=1)
    my_total = jnp.concatenate([carry[1], carry[3]], axis=1)
    stat[0] = my_top
    stat[1] = my_total
    peers = (partner, neighbour, diagonal)
    early = pl.ds(0, 2)
    stats = [
        rcopy(stat.at[early], stat_in.at[i, early], es.at[0, i], er.at[0, i], peers[i])
        for i in range(3)
    ]
    deltas_to = [
        rcopy(stat.at[2], stat_in.at[i, 2], es.at[1, i], er.at[1, i], peers[i]) for i in range(3)
    ]
    for i in (1, 2, 0):
        stats[i].start()

    def to_core(t, i):
        src = (acc, dq)[t]
        return rcopy(src.at[2 * i + 1], core_in.at[t, i], ws.at[t, i], wr.at[t, i], partner)

    def to_side(t):
        return rcopy(side_out.at[t], side_in.at[t], ws.at[t, 2], wr.at[t, 2], neighbour)

    for i in (1, 0):
        to_core(0, i).start()
    swaps[1][2].wait_recv()
    transpose_cot(1)
    my_delta = jnp.concatenate(
        [jnp.sum(do_t[i] * acc[i], axis=0, keepdims=True) for i in range(4)], axis=1
    )
    stat[2] = my_delta
    for i in (1, 2, 0):
        deltas_to[i].start()

    @pl.loop(p + 1, chips)
    def _(j):
        for kk in range(2):
            state_send(j, 0, kk).start()

    @pl.loop(0, p + 1)
    def _(j):
        for u in range(2):
            dpbuf[j, u] = mm(kv[j, 1], sdo[u], 1, 1)

    for swap in stats:
        swap.wait_recv()

    def theirs(i, row):
        return jnp.concatenate(
            [
                stat_in[i, row, :, (x ^ (i + 1)) * rows : ((x ^ (i + 1)) + 1) * rows]
                for x in range(4)
            ],
            axis=1,
        )

    top = my_top
    for i in range(3):
        top = jnp.maximum(top, theirs(i, 0))
    my_part_of = jnp.exp2(my_top - top)
    total = my_total * my_part_of
    their_part_of = [jnp.exp2(theirs(i, 0) - top) for i in range(3)]
    for i in range(3):
        total = total + theirs(i, 1) * their_part_of[i]
    inv_total = 1.0 / total

    weight = my_part_of * inv_total
    core_weight = their_part_of[0] * inv_total

    def slot_out(x):
        lanes = slice(x * rows, (x + 1) * rows)
        return acc[x] * weight[:, lanes] + core_in[0, x // 2] * core_weight[:, lanes]

    to_core(0, 1).wait_recv()
    side_out[0] = slot_out(2).astype(BF)
    to_side(0).start()

    delta = my_delta * my_part_of
    for i in range(3):
        deltas_to[i].wait_recv()
        delta = delta + theirs(i, 2) * their_part_of[i]
    delta = delta * inv_total

    def halves(v):
        return v[:, :both_rows], v[:, both_rows:]

    tops_final, inv_totals, deltas = halves(top), halves(inv_total), halves(delta)

    piece = key_rows // groups

    def to_owner(t, j, i):
        q = (group + i) % groups
        return rcopy(
            g.at[t, j, q], rin.at[t, p, group], grs.at[t, j, q], grr.at[t, p, group],
            (j * 2 + k, q * 2 + side if head_sum else h),
        )

    def from_owner(t, j, i):
        q = (group + i) % groups
        return rcopy(
            g.at[t, j, q], rin.at[t, j, q], grs.at[t, j, q], grr.at[t, j, q], partner
        )

    def put(t, j, v):
        for q in range(groups):
            g[t, j, q] = v[q * piece : (q + 1) * piece].astype(BF)

    def value_term(j):
        v = 0.0
        for u in range(2):
            prob = sbuf[j, u] * (jnp.exp2(tops[j, u] - tops_final[u]) * inv_totals[u])
            v = v + mm(prob.astype(BF), sdo[u], 1, 0)
        return v

    def key_term(j):
        v = 0.0
        for u in range(2):
            scale = jnp.exp2(tops[j, u] - tops_final[u]) * (inv_totals[u] * inv)
            ds = (sbuf[j, u] * scale * (dpbuf[j, u] - deltas[u])).astype(BF)
            dsb[u] = ds
            v = v + mm(ds, sq[u], 1, 0)
        return v

    def query_term(j):
        for u in range(2):
            term = mm(kv[j, 0], dsb[u], 0, 0)
            for i in range(2):
                dq[2 * u + i] += term[:, i * rows : (i + 1) * rows]

    dq[...] = jnp.zeros_like(dq)

    terms = ((1, value_term), (0, key_term))

    def send_term(t, j, term):
        put(t, j, term(j))
        for i in range(groups - 1, -1, -1):
            to_owner(t, j, i).start()

    def send_own(t, term):
        mine = term(p)
        for q in range(groups):
            g_own[t, q] = mine[q * piece : (q + 1) * piece]
        put(t, p, mine)
        for i in range(1, groups):
            to_owner(t, p, i).start()

    @pl.when(p >= 1)
    def _():
        for t, term in terms:
            send_term(t, 0, term)
        query_term(0)

    for t, term in terms:

        @pl.loop(1, p)
        def _(j, t=t, term=term):
            send_term(t, j, term)
            if t == 0:
                query_term(j)

    for t, term in terms:
        send_own(t, term)
    query_term(p)

    for i in (1, 0):
        to_core(1, i).start()

    def owned(t):
        total = g_own[t, group]
        for i in range(1, groups):
            from_owner(t, p, i).wait_recv()
            total = total + rin[t, p, (group + i) % groups].astype(F32)

        def add_grad(j, v):
            for i in range(groups):
                from_owner(t, j, i).wait_recv()
                v = v + rin[t, j, (group + i) % groups].astype(F32)
            return v

        return lax.fori_loop(p + 1, chips, add_grad, total)

    to_core(1, 1).wait_recv()
    side_out[1] = (dq[2] + core_in[1, 1]).astype(BF)
    to_side(1).start()

    kf = jnp.where(k == 1, 1.0, 0.0).astype(F32)
    prefix = st_par[0].astype(F32) * kf
    suffix = st_par[1].astype(F32) * (1.0 - kf)

    def add_state(j, v):
        for kk in range(2):
            state_recv(j, kk).wait_recv()
        return v + st_all[j].astype(F32)

    prefix = lax.fori_loop(0, p, add_state, prefix).astype(BF)
    suffix = lax.fori_loop(p + 1, chips, add_state, suffix).astype(BF)
    o[0] = (row_scale * (lin_acc[0] + mm(lq[...], prefix, 1, 0))).astype(BF)
    o[1] = (lin_acc[1] + mm(scot, prefix, 1, 1)).astype(BF)
    o[2] = (lin_acc[2] + mm(lv[...], suffix, 1, 1)).astype(BF)
    o[3] = (lin_acc[3] + mm(lk[...], suffix, 1, 0)).astype(BF)

    def finish(t):
        to_core(t, 0).wait_recv()
        to_side(t).wait_recv()
        out = dq[0] + core_in[1, 0] if t else slot_out(0)
        o[4 + t] = (out + side_in[t].astype(F32)).T.astype(BF)

    if head_sum:

        def result_to(t, i):
            q = (h + i) % m
            return rcopy(fq.at[t], fin.at[t, h], fs.at[t, q], fr.at[t, h], (c, q))

        def result_from(t, i):
            q = (h + i) % m
            return rcopy(fq.at[t], fin.at[t, q], fs.at[t, q], fr.at[t, q], (c, q))

        for t in (1, 0):
            fq[t] = owned(t).astype(BF)
            for i in range(1, m):
                result_to(t, i).start()
            fin[t, h] = fq[t]
        for t in range(2):
            finish(t)
        for t in (1, 0):
            for i in range(1, m):
                result_from(t, i).wait_recv()
            for q in range(m):
                start = (q % 2) * key_rows + (q // 2) * piece
                o[6 + t, start : start + piece] = fin[t, q]
        for t in (1, 0):
            for i in range(1, groups):
                to_owner(t, p, i).wait_send()
            for i in range(1, m):
                result_to(t, i).wait_send()
    else:
        o_sd[...] = jnp.zeros_like(o_sd)
        for t in (1, 0):
            o_sd[t, half] = owned(t)
        for t in range(2):
            finish(t)

    for t in range(2):
        for swap in swaps[t]:
            swap.wait_send()
        for i in range(2):
            to_core(t, i).wait_send()
        to_side(t).wait_send()
    for swap in stats + deltas_to:
        swap.wait_send()

    @pl.loop(0, p)
    def _(j):
        for kk in range(2):
            state_send(j, 1, kk).wait_send()
        for t in range(2):
            for i in range(groups):
                to_owner(t, j, i).wait_send()

    @pl.loop(p + 1, chips)
    def _(j):
        for t in range(2):
            to_chip(j, t).wait_send()
        for kk in range(2):
            state_send(j, 0, kk).wait_send()


def body(n, m, lin_q, lin_k, lin_v, lin_do, soft_q, soft_k, soft_v, soft_do, tile_list, tile_count):
    rows, d = lin_q.shape
    chips = n // 2
    head_sum = rows % (16 * m) == 0
    vmem = pl.BlockSpec(memory_space=pltpu.VMEM)
    hbm = pl.BlockSpec(memory_space=pltpu.HBM)
    if head_sum:
        out_shape = (pltpu.VMEM((8, rows, d), BF),)
    else:
        out_shape = (pltpu.VMEM((6, rows, d), BF), pltpu.VMEM((2, rows, d), F32))
    args = [
        pltpu.with_memory_space_constraint(x, pltpu.HBM)
        for x in (
            lin_q, lin_k, lin_v, lin_do, soft_q, soft_k, soft_v, soft_do, tile_list, tile_count
        )
    ]
    one = pltpu.VMEM((rows, d), BF)
    pair = pltpu.VMEM((2, 2 * rows, d), BF)
    kr = rows // 2
    groups = m // 2 if head_sum else 1
    pr = rows // m if head_sum else 16
    dma = pltpu.SemaphoreType.DMA
    outs = pl.pallas_call(
        functools.partial(layer_kernel, n, m, head_sum),
        name="layer",
        out_shape=out_shape,
        in_specs=[hbm] * 10,
        out_specs=(vmem,) * len(out_shape),
        scratch_shapes=[
            one, one, one, one, pair, pair,
            pltpu.SMEM(tile_list.shape, jnp.int32),
            pltpu.SMEM(tile_count.shape, jnp.int32),
            pltpu.VMEM((chips, 2, kr, d), BF),
            pltpu.VMEM((chips, 2, kr, 2 * rows), F32),
            pltpu.VMEM((chips, 2, kr, 2 * rows), F32),
            pltpu.VMEM((2, kr, 2 * rows), BF),
            pltpu.VMEM((2, kr, 2 * rows), BF),
            pltpu.VMEM((4, d, rows), F32),
            pltpu.VMEM((2, d, d), BF),
            pltpu.VMEM((2, d, d), BF),
            pltpu.VMEM((2, d, d), BF),
            pltpu.VMEM((chips, d, d), BF),
            pltpu.VMEM((4, rows, d), F32),
            pltpu.VMEM((2, chips, groups, kr // groups, d), BF),
            pltpu.VMEM((2, chips, groups, kr // groups, d), BF),
            pltpu.VMEM((4, d, rows), F32),
            pltpu.VMEM((4, d, rows), F32),
            pltpu.VMEM((2, 2, d, rows), F32),
            pltpu.VMEM((2, d, rows), BF),
            pltpu.VMEM((2, d, rows), BF),
            pltpu.VMEM((3, 1, 4 * rows), F32),
            pltpu.VMEM((3, 3, 1, 4 * rows), F32),
            pltpu.VMEM((2, groups, kr // groups, d), F32),
            pltpu.VMEM((2, pr, d), BF),
            pltpu.VMEM((2, m, pr, d), BF),
            pltpu.VMEM((chips, 2, 1, 2 * rows), F32),
            dma((10,)),
            dma((chips, 2)), dma((chips, 2)), dma((2, 3)), dma((2, 3)),
            dma((2, 3)), dma((2, 3)), dma((2, 3)), dma((2, 3)),
            dma, dma,
            dma((chips, 2)), dma((chips, 2)),
            dma((2, chips, groups)), dma((2, chips, groups)), dma((2, m)), dma((2, m)),
        ],
        compiler_params=pltpu.CompilerParams(
            collective_id=0, has_side_effects=True, vmem_limit_bytes=40 << 20
        ),
    )(*args)
    if head_sum:
        return tuple(outs[0][i] for i in range(8))
    soft_d = lax.psum(outs[1], "head").astype(BF)
    return tuple(outs[0][i] for i in range(6)) + (soft_d[0], soft_d[1])


def solution(mesh):
    n, m = mesh.shape["ctx"], mesh.shape["head"]
    both = P("ctx", "head")
    seq = P("ctx", None)
    return jax.shard_map(
        functools.partial(body, n, m),
        mesh=mesh,
        in_specs=(both, both, both, both, both, seq, seq, both, P(), P()),
        out_specs=(both,) * 6 + (seq, seq),
        check_vma=False,
    )
```

```python
import functools
import math

import jax
import jax.numpy as jnp
from jax import lax
from jax.experimental import pallas as pl
from jax.experimental.pallas import tpu as pltpu
from jax.sharding import PartitionSpec as P

TILE = 128
BF = jnp.bfloat16
F32 = jnp.float32
MESH = pl.DeviceIdType.MESH


def mm(a, b, da, db):
    return lax.dot_general(a, b, (((da,), (db,)), ((), ())), preferred_element_type=F32)


def layer_kernel(
    n, m, head_sum,
    lq_in, lk_in, lv_in, ldo_in, sq_in, sk_in, sv_in, sdo_in, tl_in, tc_in,
    *refs,
):
    if head_sum:
        o, *refs = refs
    else:
        o, o_sd, *refs = refs
    (
        lq, lk, lv, ldo, sq, sdo, tl, tc, kv, sbuf, dpbuf, dsb, ebuf, do_t, st_own, st_par, st_half,
        st_all, lin_acc, g, rin, acc, dq, core_in, side_out, side_in, stat, stat_in, g_own,
        fq, fin, tops, ins,
        kvs, kvr, qs, qr, es, er, ws, wr, xs, xr, hs, hr, grs, grr, fs, fr,
    ) = refs
    rows, d = lq.shape
    chips = n // 2
    c = lax.axis_index("ctx")
    h = lax.axis_index("head")
    p = c // 2
    k = c % 2
    other = 1 - k
    side = h % 2
    h2 = h + 1 - 2 * side
    partner = (p * 2 + other, h)
    neighbour = (c, h2)
    diagonal = (p * 2 + other, h2)
    key_rows = rows // 2
    half = pl.ds(pl.multiple_of(side * key_rows, key_rows), key_rows)
    first = pl.ds(0, rows)
    second = pl.ds(rows, rows)
    loads = []
    for i, (a, b) in enumerate((
        (sk_in.at[half], kv.at[p, 0]), (sv_in.at[half], kv.at[p, 1]),
        (sq_in, sq.at[0, first]), (sdo_in, sdo.at[0, first]),
        (lk_in, lk), (lv_in, lv), (lq_in, lq), (ldo_in, ldo), (tl_in, tl), (tc_in, tc),
    )):
        loads.append(pltpu.make_async_copy(a, b, ins.at[i]))
    inv = 1.0 / math.sqrt(d)

    def rcopy(src, dst, s, r, dev):
        return pltpu.make_async_remote_copy(
            src_ref=src, dst_ref=dst, send_sem=s, recv_sem=r, device_id=dev, device_id_type=MESH
        )

    for load in loads:
        load.start()
    barrier = pltpu.get_barrier_semaphore()
    greet = [((c + i) % n, h) for i in range(1, n)] + [diagonal]
    groups = m // 2 if head_sum else 1
    group = h // 2 if head_sum else 0
    greet += [(c, (h + i) % m) for i in range(1, m)] if head_sum else [neighbour]
    greet += [
        ((p + i) % chips * 2 + k, (group + q) % groups * 2 + side)
        for i in range(1, chips)
        for q in range(1, groups)
    ]
    for device in greet:
        pl.semaphore_signal(barrier, inc=1, device_id=device, device_id_type=MESH)

    for load in loads[4:8]:
        load.wait()
    pos = (c * rows + lax.broadcasted_iota(jnp.int32, (rows, d), 0) + 1).astype(F32)
    row_scale = 1.0 / jnp.sqrt(d * pos)
    scot = (ldo[...].astype(F32) * row_scale).astype(BF)
    st_own[0] = mm(lk[...], lv[...], 0, 0).astype(BF)
    st_own[1] = mm(lq[...], scot, 0, 0).astype(BF)
    for load in loads[:4] + loads[8:]:
        load.wait()
    blocks = rows // TILE
    bits = []
    for seg in (c, p * 2 + other):
        for b in range(blocks):
            row = seg * blocks + b
            word = jnp.int32(0)
            for s in range(tl.shape[1]):
                bit = lax.shift_left(jnp.int32(1), tl[row, s])
                word = word | jnp.where(s < tc[row], bit, 0)
            bits.append(word)
    pl.semaphore_wait(barrier, len(greet))

    def to_chip(j, t):
        return rcopy(kv.at[p, t], kv.at[p, t], kvs.at[j, t], kvr.at[p, t], (j * 2 + k, h))

    def from_chip(j, t):
        return rcopy(kv.at[p, t], kv.at[j, t], kvs.at[j, t], kvr.at[j, t], (j * 2 + k, h))

    def query_copies(buf, t):
        return (
            rcopy(buf.at[0, first], buf.at[1, first], qs.at[t, 0], qr.at[t, 0], neighbour),
            rcopy(buf.at[0, first], buf.at[0, second], qs.at[t, 1], qr.at[t, 1], partner),
            rcopy(buf.at[1, first], buf.at[1, second], qs.at[t, 2], qr.at[t, 2], partner),
        )

    swaps = (query_copies(sq, 0), query_copies(sdo, 1))
    swaps[0][0].start()

    @pl.loop(p + 1, chips)
    def _(i):
        j = chips - (i - p)
        to_chip(j, 0).start()
        to_chip(j, 1).start()

    swaps[0][1].start()
    swaps[1][1].start()
    exchange = rcopy(st_own, st_par, xs, xr, partner)
    exchange.start()

    tri = lax.broadcasted_iota(jnp.int32, (rows, rows), 0) >= lax.broadcasted_iota(
        jnp.int32, (rows, rows), 1
    )
    aqk = jnp.where(tri, mm(lq[...], lk[...], 1, 1), 0.0).astype(BF)
    adv = jnp.where(tri, mm(scot, lv[...], 1, 1), 0.0).astype(BF)
    lin_acc[0] = mm(aqk, lv[...], 1, 0)
    lin_acc[1] = mm(adv, lk[...], 1, 0)
    lin_acc[2] = mm(adv, lq[...], 0, 0)
    lin_acc[3] = mm(aqk, scot, 0, 0)
    swaps[1][0].start()

    exchange.wait()
    st_half[...] = (st_own[...].astype(F32) + st_par[...].astype(F32)).astype(BF)
    hd = d // 2
    my_part = pl.ds(pl.multiple_of(k * hd, hd), hd)

    def state_send(j, t, kk):
        return rcopy(
            st_half.at[t, my_part], st_all.at[p, my_part], hs.at[j, kk], hr.at[p, k],
            (j * 2 + kk, h),
        )

    def state_recv(j, kk):
        part = pl.ds(kk * hd, hd)
        return rcopy(
            st_half.at[0, part], st_all.at[j, part], hs.at[j, kk], hr.at[j, kk], partner
        )

    @pl.loop(0, p)
    def _(j):
        for kk in range(2):
            state_send(j, 1, kk).start()

    both_rows = 2 * rows
    key_blocks = key_rows // TILE
    lane_block = lax.broadcasted_iota(jnp.int32, (1, both_rows), 1) // TILE
    factor = inv * math.log2(math.e)

    def fold(j, sides, carry, own, wait):
        if wait:
            from_chip(j, 0).wait_recv()
        biases = []
        for i in range(key_blocks):
            kb = (j * 2 + k) * blocks + side * key_blocks + i
            bias = jnp.zeros((1, both_rows), F32)
            for b in range(2 * blocks):
                live = lax.shift_right_logical(bits[b], kb) & 1
                bias = jnp.where(lane_block == b, jnp.where(live == 1, 0.0, -1e30), bias)
            biases.append(bias)
        tops_here, totals = list(carry[0::2]), list(carry[1::2])
        alphas = []
        for x, u in enumerate(sides):
            new_top = tops_here[x]
            for i in range(key_blocks):
                part = pl.ds(i * TILE, TILE)
                s = mm(kv[j, 0, part], sq[u], 1, 1)
                if own:
                    key = (
                        k * rows + side * key_rows + i * TILE
                        + lax.broadcasted_iota(jnp.int32, s.shape, 0)
                    )
                    lane = lax.broadcasted_iota(jnp.int32, s.shape, 1)
                    query = jnp.where(lane < rows, k * rows + lane, other * rows + lane - rows)
                    s = jnp.where(key <= query, s, -1e30)
                sbuf[j, u, part] = s
                top_here = jnp.max(s, axis=0, keepdims=True) * factor + biases[i]
                new_top = jnp.maximum(new_top, top_here)
            alphas.append(jnp.exp2(tops_here[x] - new_top))
            tops_here[x] = new_top
            tops[j, u] = new_top
        if wait:
            from_chip(j, 1).wait_recv()
        for x, u in enumerate(sides):
            total = totals[x] * alphas[x]
            for i in range(key_blocks):
                part = pl.ds(i * TILE, TILE)
                e = jnp.exp2(sbuf[j, u, part] * factor + (biases[i] - tops_here[x]))
                sbuf[j, u, part] = e
                ebuf[u, part] = e.astype(BF)
                total = total + jnp.sum(e, axis=0, keepdims=True)
            totals[x] = total
            term = mm(kv[j, 1], ebuf[u], 0, 0)
            for i in range(2):
                lanes = slice(i * rows, (i + 1) * rows)
                if own:
                    acc[2 * u + i] = term[:, lanes]
                else:
                    acc[2 * u + i] = acc[2 * u + i] * alphas[x][:, lanes] + term[:, lanes]
        return tuple(v for pair in zip(tops_here, totals) for v in pair)

    def transpose_cot(u):
        for i in range(2):
            do_t[2 * u + i] = sdo[u, i * rows : (i + 1) * rows].astype(F32).T

    empty = (jnp.full((1, both_rows), -3e30, F32), jnp.zeros((1, both_rows), F32))
    near = jnp.minimum(p, 1) + 1
    swaps[0][1].wait_recv()
    mine = fold(p, (0,), empty, True, False)
    swaps[1][1].wait_recv()
    transpose_cot(0)
    swaps[0][0].wait_recv()
    swaps[0][2].start()
    mine = lax.fori_loop(1, near, lambda i, v: fold(p - i, (0,), v, False, True), mine)
    swaps[1][0].wait_recv()
    swaps[1][2].start()
    swaps[0][2].wait_recv()
    side_carry = fold(p, (1,), empty, True, False)
    side_carry = lax.fori_loop(
        1, near, lambda i, v: fold(p - i, (1,), v, False, False), side_carry
    )

    def fold_both(i, v):
        return fold(p - i, (0, 1), v, False, True)

    carry = lax.fori_loop(near, p + 1, fold_both, mine + side_carry)
    my_top = jnp.concatenate([carry[0], carry[2]], axis=1)
    my_total = jnp.concatenate([carry[1], carry[3]], axis=1)
    stat[0] = my_top
    stat[1] = my_total
    peers = (partner, neighbour, diagonal)
    early = pl.ds(0, 2)
    stats = [
        rcopy(stat.at[early], stat_in.at[i, early], es.at[0, i], er.at[0, i], peers[i])
        for i in range(3)
    ]
    deltas_to = [
        rcopy(stat.at[2], stat_in.at[i, 2], es.at[1, i], er.at[1, i], peers[i]) for i in range(3)
    ]
    for i in (1, 2, 0):
        stats[i].start()

    def to_core(t, i):
        src = (acc, dq)[t]
        return rcopy(src.at[2 * i + 1], core_in.at[t, i], ws.at[t, i], wr.at[t, i], partner)

    def to_side(t):
        return rcopy(side_out.at[t], side_in.at[t], ws.at[t, 2], wr.at[t, 2], neighbour)

    for i in (1, 0):
        to_core(0, i).start()
    swaps[1][2].wait_recv()
    transpose_cot(1)
    my_delta = jnp.concatenate(
        [jnp.sum(do_t[i] * acc[i], axis=0, keepdims=True) for i in range(4)], axis=1
    )
    stat[2] = my_delta
    for i in (1, 2, 0):
        deltas_to[i].start()

    @pl.loop(p + 1, chips)
    def _(j):
        for kk in range(2):
            state_send(j, 0, kk).start()

    @pl.loop(0, p + 1)
    def _(j):
        for u in range(2):
            dpbuf[j, u] = mm(kv[j, 1], sdo[u], 1, 1)

    for swap in stats:
        swap.wait_recv()

    def theirs(i, row):
        return jnp.concatenate(
            [
                stat_in[i, row, :, (x ^ (i + 1)) * rows : ((x ^ (i + 1)) + 1) * rows]
                for x in range(4)
            ],
            axis=1,
        )

    top = my_top
    for i in range(3):
        top = jnp.maximum(top, theirs(i, 0))
    my_part_of = jnp.exp2(my_top - top)
    total = my_total * my_part_of
    their_part_of = [jnp.exp2(theirs(i, 0) - top) for i in range(3)]
    for i in range(3):
        total = total + theirs(i, 1) * their_part_of[i]
    inv_total = 1.0 / total

    weight = my_part_of * inv_total
    core_weight = their_part_of[0] * inv_total

    def slot_out(x):
        lanes = slice(x * rows, (x + 1) * rows)
        return acc[x] * weight[:, lanes] + core_in[0, x // 2] * core_weight[:, lanes]

    def halves(v):
        return v[:, :both_rows], v[:, both_rows:]

    tops_final, inv_totals = halves(top), halves(inv_total)

    piece = key_rows // groups

    def to_owner(t, j, i):
        q = (group + i) % groups
        return rcopy(
            g.at[t, j, q], rin.at[t, p, group], grs.at[t, j, q], grr.at[t, p, group],
            (j * 2 + k, q * 2 + side if head_sum else h),
        )

    def from_owner(t, j, i):
        q = (group + i) % groups
        return rcopy(
            g.at[t, j, q], rin.at[t, j, q], grs.at[t, j, q], grr.at[t, j, q], partner
        )

    def put(t, j, v):
        for q in range(groups):
            g[t, j, q] = v[q * piece : (q + 1) * piece].astype(BF)

    def value_term(j):
        v = 0.0
        for u in range(2):
            prob = sbuf[j, u] * (jnp.exp2(tops[j, u] - tops_final[u]) * inv_totals[u])
            v = v + mm(prob.astype(BF), sdo[u], 1, 0)
        return v

    def key_term(j, deltas):
        v = 0.0
        for u in range(2):
            scale = jnp.exp2(tops[j, u] - tops_final[u]) * (inv_totals[u] * inv)
            ds = (sbuf[j, u] * scale * (dpbuf[j, u] - deltas[u])).astype(BF)
            dsb[u] = ds
            v = v + mm(ds, sq[u], 1, 0)
        return v

    def query_term(j):
        for u in range(2):
            term = mm(kv[j, 0], dsb[u], 0, 0)
            for i in range(2):
                dq[2 * u + i] += term[:, i * rows : (i + 1) * rows]

    dq[...] = jnp.zeros_like(dq)


    def send_term(t, j, term):
        put(t, j, term(j))
        for i in range(groups - 1, -1, -1):
            to_owner(t, j, i).start()

    def send_own(t, term):
        mine = term(p)
        for q in range(groups):
            g_own[t, q] = mine[q * piece : (q + 1) * piece]
        put(t, p, mine)
        for i in range(1, groups):
            to_owner(t, p, i).start()

    @pl.when(p >= 1)
    def _():
        send_term(1, 0, value_term)

    delta = my_delta * my_part_of
    for i in range(3):
        deltas_to[i].wait_recv()
        delta = delta + theirs(i, 2) * their_part_of[i]
    delta = delta * inv_total

    deltas = halves(delta)
    terms = ((1, value_term), (0, lambda j: key_term(j, deltas)))

    @pl.when(p >= 1)
    def _():
        send_term(0, 0, terms[1][1])
        query_term(0)

    to_core(0, 1).wait_recv()
    side_out[0] = slot_out(2).astype(BF)
    to_side(0).start()

    for t, term in terms:

        @pl.loop(1, p)
        def _(j, t=t, term=term):
            send_term(t, j, term)
            if t == 0:
                query_term(j)

    for t, term in terms:
        send_own(t, term)
    query_term(p)

    for i in (1, 0):
        to_core(1, i).start()

    def owned(t):
        total = g_own[t, group]
        for i in range(1, groups):
            from_owner(t, p, i).wait_recv()
            total = total + rin[t, p, (group + i) % groups].astype(F32)

        def add_grad(j, v):
            for i in range(groups):
                from_owner(t, j, i).wait_recv()
                v = v + rin[t, j, (group + i) % groups].astype(F32)
            return v

        return lax.fori_loop(p + 1, chips, add_grad, total)

    to_core(1, 1).wait_recv()
    side_out[1] = (dq[2] + core_in[1, 1]).astype(BF)
    to_side(1).start()

    kf = jnp.where(k == 1, 1.0, 0.0).astype(F32)
    prefix = st_par[0].astype(F32) * kf
    suffix = st_par[1].astype(F32) * (1.0 - kf)

    def add_state(j, v):
        for kk in range(2):
            state_recv(j, kk).wait_recv()
        return v + st_all[j].astype(F32)

    prefix = lax.fori_loop(0, p, add_state, prefix).astype(BF)
    suffix = lax.fori_loop(p + 1, chips, add_state, suffix).astype(BF)
    o[0] = (row_scale * (lin_acc[0] + mm(lq[...], prefix, 1, 0))).astype(BF)
    o[1] = (lin_acc[1] + mm(scot, prefix, 1, 1)).astype(BF)
    o[2] = (lin_acc[2] + mm(lv[...], suffix, 1, 1)).astype(BF)
    o[3] = (lin_acc[3] + mm(lk[...], suffix, 1, 0)).astype(BF)

    def finish(t):
        to_core(t, 0).wait_recv()
        to_side(t).wait_recv()
        out = dq[0] + core_in[1, 0] if t else slot_out(0)
        o[4 + t] = (out + side_in[t].astype(F32)).T.astype(BF)

    if head_sum:

        def result_to(t, q):
            return rcopy(fq.at[t], fin.at[t, h], fs.at[t, q], fr.at[t, h], (c, q))

        def result_from(t, i):
            q = (h + i) % m
            return rcopy(fq.at[t], fin.at[t, q], fs.at[t, q], fr.at[t, q], (c, q))

        for t in (1, 0):
            fq[t] = owned(t).astype(BF)
            for q in range(m):
                pl.when(q != h)(lambda t=t, q=q: result_to(t, q).start())
            fin[t, h] = fq[t]
        for t in range(2):
            finish(t)
        for t in (1, 0):
            for i in range(1, m):
                result_from(t, i).wait_recv()
            for q in range(m):
                start = (q % 2) * key_rows + (q // 2) * piece
                o[6 + t, start : start + piece] = fin[t, q]
        for t in (1, 0):
            for i in range(1, groups):
                to_owner(t, p, i).wait_send()
            for i in range(1, m):
                result_to(t, (h + i) % m).wait_send()
    else:
        o_sd[...] = jnp.zeros_like(o_sd)
        for t in (1, 0):
            o_sd[t, half] = owned(t)
        for t in range(2):
            finish(t)

    for t in range(2):
        for swap in swaps[t]:
            swap.wait_send()
        for i in range(2):
            to_core(t, i).wait_send()
        to_side(t).wait_send()
    for swap in stats + deltas_to:
        swap.wait_send()

    @pl.loop(0, p)
    def _(j):
        for kk in range(2):
            state_send(j, 1, kk).wait_send()
        for t in range(2):
            for i in range(groups):
                to_owner(t, j, i).wait_send()

    @pl.loop(p + 1, chips)
    def _(j):
        for t in range(2):
            to_chip(j, t).wait_send()
        for kk in range(2):
            state_send(j, 0, kk).wait_send()


def body(n, m, lin_q, lin_k, lin_v, lin_do, soft_q, soft_k, soft_v, soft_do, tile_list, tile_count):
    rows, d = lin_q.shape
    chips = n // 2
    head_sum = rows % (16 * m) == 0
    vmem = pl.BlockSpec(memory_space=pltpu.VMEM)
    hbm = pl.BlockSpec(memory_space=pltpu.HBM)
    if head_sum:
        out_shape = (pltpu.VMEM((8, rows, d), BF),)
    else:
        out_shape = (pltpu.VMEM((6, rows, d), BF), pltpu.VMEM((2, rows, d), F32))
    args = [
        pltpu.with_memory_space_constraint(x, pltpu.HBM)
        for x in (
            lin_q, lin_k, lin_v, lin_do, soft_q, soft_k, soft_v, soft_do, tile_list, tile_count
        )
    ]
    one = pltpu.VMEM((rows, d), BF)
    pair = pltpu.VMEM((2, 2 * rows, d), BF)
    kr = rows // 2
    groups = m // 2 if head_sum else 1
    pr = rows // m if head_sum else 16
    dma = pltpu.SemaphoreType.DMA
    outs = pl.pallas_call(
        functools.partial(layer_kernel, n, m, head_sum),
        name="layer",
        out_shape=out_shape,
        in_specs=[hbm] * 10,
        out_specs=(vmem,) * len(out_shape),
        scratch_shapes=[
            one, one, one, one, pair, pair,
            pltpu.SMEM(tile_list.shape, jnp.int32),
            pltpu.SMEM(tile_count.shape, jnp.int32),
            pltpu.VMEM((chips, 2, kr, d), BF),
            pltpu.VMEM((chips, 2, kr, 2 * rows), F32),
            pltpu.VMEM((chips, 2, kr, 2 * rows), F32),
            pltpu.VMEM((2, kr, 2 * rows), BF),
            pltpu.VMEM((2, kr, 2 * rows), BF),
            pltpu.VMEM((4, d, rows), F32),
            pltpu.VMEM((2, d, d), BF),
            pltpu.VMEM((2, d, d), BF),
            pltpu.VMEM((2, d, d), BF),
            pltpu.VMEM((chips, d, d), BF),
            pltpu.VMEM((4, rows, d), F32),
            pltpu.VMEM((2, chips, groups, kr // groups, d), BF),
            pltpu.VMEM((2, chips, groups, kr // groups, d), BF),
            pltpu.VMEM((4, d, rows), F32),
            pltpu.VMEM((4, d, rows), F32),
            pltpu.VMEM((2, 2, d, rows), F32),
            pltpu.VMEM((2, d, rows), BF),
            pltpu.VMEM((2, d, rows), BF),
            pltpu.VMEM((3, 1, 4 * rows), F32),
            pltpu.VMEM((3, 3, 1, 4 * rows), F32),
            pltpu.VMEM((2, groups, kr // groups, d), F32),
            pltpu.VMEM((2, pr, d), BF),
            pltpu.VMEM((2, m, pr, d), BF),
            pltpu.VMEM((chips, 2, 1, 2 * rows), F32),
            dma((10,)),
            dma((chips, 2)), dma((chips, 2)), dma((2, 3)), dma((2, 3)),
            dma((2, 3)), dma((2, 3)), dma((2, 3)), dma((2, 3)),
            dma, dma,
            dma((chips, 2)), dma((chips, 2)),
            dma((2, chips, groups)), dma((2, chips, groups)), dma((2, m)), dma((2, m)),
        ],
        compiler_params=pltpu.CompilerParams(
            collective_id=0, has_side_effects=True, vmem_limit_bytes=40 << 20
        ),
    )(*args)
    if head_sum:
        return tuple(outs[0][i] for i in range(8))
    soft_d = lax.psum(outs[1], "head").astype(BF)
    return tuple(outs[0][i] for i in range(6)) + (soft_d[0], soft_d[1])


def solution(mesh):
    n, m = mesh.shape["ctx"], mesh.shape["head"]
    both = P("ctx", "head")
    seq = P("ctx", None)
    return jax.shard_map(
        functools.partial(body, n, m),
        mesh=mesh,
        in_specs=(both, both, both, both, both, seq, seq, both, P(), P()),
        out_specs=(both,) * 6 + (seq, seq),
        check_vma=False,
    )
```
